32 devices in a mesh: chan: 16 (over z, x, core), rows: 2 (over y).
Axes of the slice: x: 2, y: 2, z: 4, core: 2. Of those that a mesh axis runs over, the one named last changes fastest.
Arguments:
- image: bfloat16 [768, 1, 32, 128], P('chan', None, 'rows'), may hold values from -3 to 3
- dw_kernel: float32 [768, 7, 7], P('chan'), may hold values from -13 to 13
- ln_gain: float32 [768], P('chan'), may hold values from 0.1 to 1.9
- w_in: bfloat16 [768, 3072], P(None, 'chan'), may hold values from -0.21875 to 0.21875
- w_out: bfloat16 [3072, 768], P('chan'), may hold values from -0.15625 to 0.15625
- layer_scale: float32 [768], P('chan'), may hold values from 0.3 to 1
- cotangent: bfloat16 [768, 1, 32, 128], P('chan', None, 'rows'), may hold values from -6 to 6
Outputs:
- block_out: bfloat16 [768, 1, 32, 128], P('chan', None, 'rows')
- grad_image: bfloat16 [768, 1, 32, 128], P('chan', None, 'rows')
- grad_kernel: float32 [768, 7, 7], P('chan')
- grad_gain: float32 [768], P('chan')
- grad_scale: float32 [768], P('chan')
- grad_w_in: float32 [768, 3072], P(None, 'chan')
- grad_w_out: float32 [3072, 768], P('chan')
The draws below stay inside these ranges and needn't reach their ends.
All inputs are finite; a program needn't handle non-finite values.
Results may differ from the reference program's by a relative error of at most 0.018.
Values may be sent and summed in bfloat16 or wider, within the bound.
A program may use at most 64 MiB of HBM per device.

```python
import math
import jax
import jax.numpy as jnp
from jax import lax

D = 768
HID = 3072
KSIZE = 7
IMGS = 1
WID = 128
HGT = 32
N_CHAN = 16


def draw_dw_kernel(key, part):
    key_scale = jax.random.fold_in(key, 11)
    key_base = jax.random.fold_in(key, 23)
    channel = jnp.arange(D, dtype=jnp.float32)
    ramp = 3.0 ** (channel / (D - 1))
    spread = 10.0 ** jax.random.uniform(key_scale, (D,), jnp.float32, 0.0, 1.0)
    base = jax.random.truncated_normal(key_base, -3.0, 3.0, (D, KSIZE, KSIZE), jnp.float32)
    return (base * (ramp * spread / 7.0)[:, None, None]).astype(jnp.float32)


def with_spikes(drawn, own_key, source, target, shards_of, factor):
    owner, partner = [(jnp.arange(drawn.shape[position]) // (drawn.shape[position] // shards_of)).reshape([-1 if axis == position else 1 for axis in range(drawn.ndim)]) for position in (source, target)]
    chosen = jax.random.permutation(own_key, shards_of)[partner]
    strong = (owner == chosen) | (owner == (partner + shards_of // 2) % shards_of)
    return jnp.where(strong, factor * drawn, drawn)


def level_of(key, extent, pieces, least, largest):
    def one(axis_at, blocks):
        draws = jax.random.uniform(jax.random.fold_in(jax.random.fold_in(key, 6), axis_at), (blocks,), jnp.float32, least / len(pieces), largest / len(pieces))
        return jnp.repeat(jnp.exp(draws), extent[axis_at] // blocks).reshape((-1,) + (1,) * (len(extent) - axis_at - 1))

    gain = one(*pieces[0])
    for cut in pieces[1:]:
        gain = gain * one(*cut)
    return gain


def scatter_about(rng, dims, deviation, limit, shards=(), kind=jnp.bfloat16):
    factor_of = level_of(rng, dims, shards, -0.22, 0.18) if shards else 1.0
    values = jax.random.normal(rng, dims, jnp.float32) * deviation * factor_of
    return jnp.minimum(jnp.maximum(values, -limit), limit).astype(kind)


def heavy_noise(key, extent, scale, reach, cuts, heavy, kind=jnp.bfloat16):
    entries = scale * jax.random.normal(key, extent, jnp.float32)
    if cuts:
        entries = entries * level_of(key, extent, cuts, -0.22, 0.18)
    return jnp.clip(with_spikes(entries, jax.random.fold_in(key, 3), *heavy), -reach, reach).astype(kind)


def setup_inputs(seed: int = 0) -> dict:
    seeds = jax.random.split(jax.random.key(seed), 8)
    image = scatter_about(seeds[0], (D, IMGS, HGT, WID), 0.5, 3.0, ((0, 16), (2, 2)))
    dw_kernel = draw_dw_kernel(jax.random.fold_in(seeds[7], 71), 0)
    ln_gain = jnp.clip(1.0 + 0.18 * jax.random.normal(seeds[2], (D,), jnp.float32), 0.1, 1.9)
    w_in = scatter_about(seeds[3], (D, HID), D ** -0.5, 0.21875, ((1, 16),))
    w_out = heavy_noise(seeds[4], (HID, D), HID ** -0.5, 0.15625, ((0, 16),), (0, 1, 16, 2.0))
    layer_scale = jnp.clip(jnp.exp(math.log(1.0) - 1.2039728 * jax.random.uniform(seeds[5], (D,), jnp.float32) ** level_of(seeds[5], (D,), ((0, 16),), -0.2, 0.2)), 0.3, 1.0)
    cotangent = scatter_about(seeds[6], (D, IMGS, HGT, WID), 1.0, 6.0, ((0, 16), (2, 2)))
    return dict(image=image, dw_kernel=dw_kernel, ln_gain=ln_gain, w_in=w_in, w_out=w_out, layer_scale=layer_scale, cotangent=cotangent)


epsilon = 1e-06
inv_root_two = 0.7071067811865476
inv_root_two_pi = 0.3989422804014327

def gelu_slope(values):
    return 0.5 * (1.0 + lax.erf(values * inv_root_two)) + values * jnp.exp(-0.5 * values * values) * inv_root_two_pi

def forward_taps(padded, kernel, height, breadth):
    running = jnp.zeros((padded.shape[0], padded.shape[1], height, breadth), jnp.float32)
    for u in range(KSIZE):
        for v in range(KSIZE):
            running = running + kernel[:, u, v][:, None, None, None] * padded[:, :, u:u + height, v:v + breadth]
    return running

def transpose_taps(padded, kernel, height, breadth):
    running = jnp.zeros((padded.shape[0], padded.shape[1], height, breadth), jnp.float32)
    for u in range(KSIZE):
        for v in range(KSIZE):
            running = running + kernel[:, u, v][:, None, None, None] * padded[:, :, 6 - u:6 - u + height, 6 - v:6 - v + breadth]
    return running

def correlate_taps(padded, grad, height, breadth):
    columns = []
    for u in range(KSIZE):
        row_terms = []
        for v in range(KSIZE):
            row_terms.append(lax.optimization_barrier(jnp.sum(grad * padded[:, :, u:u + height, v:v + breadth], axis=(1, 2, 3))))
        columns.append(jnp.stack(row_terms, axis=1))
    return jnp.stack(columns, axis=1)

def blocked_sum(weights_blocks, data_blocks):

    def step(running, pair):
        weight_block, data_block = pair
        partial_term = jnp.dot(weight_block, data_block, preferred_element_type=jnp.float32).astype(jnp.bfloat16)
        partial_term = lax.optimization_barrier(partial_term)
        return (running + partial_term.astype(jnp.float32), None)
    start_value = jnp.zeros((weights_blocks.shape[1], data_blocks.shape[2]), jnp.float32)
    result, _ = lax.scan(step, start_value, (weights_blocks, data_blocks))
    return result

def reference(image, dw_kernel, ln_gain, w_in, w_out, layer_scale, cotangent):
    pixels = IMGS * HGT * WID
    hidden_block = HID // N_CHAN
    image_f = image.astype(jnp.float32)
    padded = jnp.pad(image_f, ((0, 0), (0, 0), (3, 3), (3, 3)))
    mixed_in = forward_taps(padded, dw_kernel, HGT, WID).astype(jnp.bfloat16)
    mixed_flat = mixed_in.reshape(D, pixels).astype(jnp.float32)
    centre = lax.optimization_barrier(jnp.mean(mixed_flat, axis=0))
    spread = lax.optimization_barrier(jnp.mean(jnp.square(mixed_flat - centre), axis=0))
    inv_scale = 1.0 / jnp.sqrt(spread + epsilon)
    unit_norm = (mixed_flat - centre) * inv_scale
    normed = (unit_norm * ln_gain[:, None]).astype(jnp.bfloat16)
    pre_act = jnp.dot(w_in.T, normed, preferred_element_type=jnp.float32)
    activated = jax.nn.gelu(pre_act, approximate=False).astype(jnp.bfloat16)
    out_blocks = jnp.transpose(w_out.reshape(N_CHAN, hidden_block, D), (0, 2, 1))
    act_blocks = activated.reshape(N_CHAN, hidden_block, pixels)
    branch = blocked_sum(out_blocks, act_blocks)
    block_out = (image_f.reshape(D, pixels) + layer_scale[:, None] * branch).astype(jnp.bfloat16)
    cotan_flat = cotangent.reshape(D, pixels).astype(jnp.float32)
    scaled = (layer_scale[:, None] * cotan_flat).astype(jnp.bfloat16)
    grad_act = jnp.dot(w_out, scaled, preferred_element_type=jnp.float32)
    grad_w_out = jnp.dot(activated, scaled.T, preferred_element_type=jnp.float32)
    grad_scale = lax.optimization_barrier(jnp.sum(cotan_flat * branch, axis=1))
    grad_pre = (grad_act * gelu_slope(pre_act)).astype(jnp.bfloat16)
    grad_w_in = jnp.dot(normed, grad_pre.T, preferred_element_type=jnp.float32)
    in_blocks = jnp.transpose(w_in.reshape(D, N_CHAN, hidden_block), (1, 0, 2))
    pre_blocks = grad_pre.reshape(N_CHAN, hidden_block, pixels)
    grad_normed = blocked_sum(in_blocks, pre_blocks)
    grad_gain = lax.optimization_barrier(jnp.sum(grad_normed * unit_norm, axis=1))
    scaled_grad = grad_normed * ln_gain[:, None]
    mean_one = lax.optimization_barrier(jnp.mean(scaled_grad, axis=0))
    mean_two = lax.optimization_barrier(jnp.mean(scaled_grad * unit_norm, axis=0))
    grad_mixed = (inv_scale * (scaled_grad - mean_one - unit_norm * mean_two)).astype(jnp.bfloat16)
    grad_four = grad_mixed.reshape(D, IMGS, HGT, WID).astype(jnp.float32)
    grad_padded = jnp.pad(grad_four, ((0, 0), (0, 0), (3, 3), (3, 3)))
    spread_back = transpose_taps(grad_padded, dw_kernel, HGT, WID)
    grad_image = (cotangent.astype(jnp.float32) + spread_back).astype(jnp.bfloat16)
    grad_kernel = correlate_taps(padded, grad_four, HGT, WID)
    return (block_out.reshape(D, IMGS, HGT, WID), grad_image, grad_kernel, grad_gain, grad_scale, grad_w_in, grad_w_out)
```

```python
import functools

import jax
import jax.numpy as jnp
from jax import lax
from jax.experimental import pallas as pl
from jax.experimental.pallas import tpu as pltpu
from jax.sharding import PartitionSpec as P

D = 768
KSIZE = 7


epsilon = 1e-06
inv_root_two = 0.7071067811865476
inv_root_two_pi = 0.3989422804014327


def extended(block, sides, width):
    for axis, dim in sides:
        count = lax.axis_size(axis)
        forward = [(i, i + 1) for i in range(count - 1)]
        backward = [(target, source) for source, target in forward]
        low = lax.ppermute(
            lax.slice_in_dim(block, block.shape[dim] - width, None, axis=dim), axis, forward
        )
        high = lax.ppermute(lax.slice_in_dim(block, 0, width, axis=dim), axis, backward)
        block = jnp.concatenate([low, block, high], axis=dim)
    return block


def gelu_slope(values):
    return (
        0.5 * (1.0 + lax.erf(values * inv_root_two))
        + values * jnp.exp(-0.5 * values * values) * inv_root_two_pi
    )


def forward_taps(padded, kernel, height, breadth):
    running = jnp.zeros((padded.shape[0], padded.shape[1], height, breadth), jnp.float32)
    for u in range(KSIZE):
        for v in range(KSIZE):
            running = (
                running
                + kernel[:, u, v][:, None, None, None]
                * padded[:, :, u : u + height, v : v + breadth]
            )
    return running


def transpose_taps(padded, kernel, height, breadth):
    running = jnp.zeros((padded.shape[0], padded.shape[1], height, breadth), jnp.float32)
    for u in range(KSIZE):
        for v in range(KSIZE):
            running = (
                running
                + kernel[:, u, v][:, None, None, None]
                * padded[:, :, 6 - u : 6 - u + height, 6 - v : 6 - v + breadth]
            )
    return running


def correlate_taps(padded, grad, height, breadth):
    columns = []
    for u in range(KSIZE):
        row_terms = []
        for v in range(KSIZE):
            row_terms.append(
                jnp.sum(grad * padded[:, :, u : u + height, v : v + breadth], axis=(1, 2, 3))
            )
        columns.append(jnp.stack(row_terms, axis=1))
    return jnp.stack(columns, axis=1)

GROUP = 4
MESH = pl.DeviceIdType.MESH


def greet(n, me):
    barrier = pltpu.get_barrier_semaphore()
    for k in range(1, n):
        pl.semaphore_signal(
            barrier, inc=1, device_id={"chan": lax.rem(me + k, n)}, device_id_type=MESH
        )
    pl.semaphore_wait(barrier, n - 1)


def spread_kernel(n, part, *refs):
    count = (len(refs) - 3) // 2
    sources, targets = refs[:count], refs[count : 2 * count]
    local_sem, send_sem, recv_sem = refs[2 * count :]
    me = lax.axis_index("chan")
    greet(n, me)

    def piece(ref, peer):
        if ref.shape[-1] == part * GROUP:
            return ref.at[:, pl.ds(pl.multiple_of(lax.rem(peer, GROUP) * part, part), part)]
        return ref

    copies = []
    for k in range(1, n):
        peer = lax.rem(me + k, n)
        for a in range(count):
            copy = pltpu.make_async_remote_copy(
                src_ref=piece(sources[a], peer),
                dst_ref=targets[a].at[me],
                send_sem=send_sem.at[a, k],
                recv_sem=recv_sem.at[a, k],
                device_id={"chan": peer},
                device_id_type=MESH,
            )
            copy.start()
            copies.append(copy)
    own = []
    for a in range(count):
        copy = pltpu.make_async_copy(piece(sources[a], me), targets[a].at[me], local_sem.at[a])
        copy.start()
        own.append(copy)
    for copy in own + copies:
        copy.wait()


def collect_kernel(n, part, *refs):
    count = (len(refs) - 3) // 2
    sources, targets = refs[:count], refs[count : 2 * count]
    local_sem, send_sem, recv_sem = refs[2 * count :]
    me = lax.axis_index("chan")
    plane = lax.div(me, GROUP)
    greet(n, me)
    columns = pl.ds(pl.multiple_of(lax.rem(me, GROUP) * part, part), part)

    def piece(ref, peer):
        return ref.at[peer] if len(ref.shape) == 3 else ref

    copies = []
    for k in range(1, n):
        peer = lax.rem(me + k, n)
        for a in range(count):
            copy = pltpu.make_async_remote_copy(
                src_ref=piece(sources[a], peer),
                dst_ref=targets[a].at[plane, :, columns],
                send_sem=send_sem.at[a, k],
                recv_sem=recv_sem.at[a, k],
                device_id={"chan": peer},
                device_id_type=MESH,
            )
            copy.start()
            copies.append(copy)
    own = []
    for a in range(count):
        copy = pltpu.make_async_copy(
            piece(sources[a], me), targets[a].at[plane, :, columns], local_sem.at[a]
        )
        copy.start()
        own.append(copy)
    for copy in own + copies:
        copy.wait()


def exchange(kernel, identity, arrays, shapes, n, part):
    count = len(arrays)
    size = sum(a.size * a.dtype.itemsize for a in arrays)
    return pl.pallas_call(
        functools.partial(kernel, n, part),
        out_shape=tuple(
            jax.ShapeDtypeStruct(shape, a.dtype) for shape, a in zip(shapes, arrays)
        ),
        in_specs=[pl.BlockSpec(memory_space=pl.ANY)] * count,
        out_specs=tuple([pl.BlockSpec(memory_space=pl.ANY)] * count),
        scratch_shapes=[
            pltpu.SemaphoreType.DMA((count,)),
            pltpu.SemaphoreType.DMA((count, n)),
            pltpu.SemaphoreType.DMA((count, n)),
        ],
        compiler_params=pltpu.CompilerParams(collective_id=identity, has_side_effects=True),
        cost_estimate=pl.CostEstimate(flops=0, bytes_accessed=100 * size, transcendentals=0),
    )(*arrays)


def swap(value, axis, bit):
    n = lax.axis_size(axis)
    return lax.ppermute(value, axis, [(i, i ^ bit) for i in range(n)])


def total_over(value, axis):
    bit = 1
    while bit < lax.axis_size(axis):
        near = value.astype(jnp.bfloat16)
        value = near.astype(jnp.float32) + swap(near, axis, bit).astype(jnp.float32)
        bit *= 2
    return value


def body(image, dw_kernel, ln_gain, w_in, w_out, layer_scale, cotangent):
    channels, images, height, breadth = image.shape
    pixels = images * height * breadth
    part = pixels // GROUP
    n = lax.axis_size("chan")
    planes = n // GROUP
    contract_lead = (((0,), (0,)), ((), ()))
    contract_tail = (((1,), (1,)), ((), ()))
    bf16, f32 = jnp.bfloat16, jnp.float32
    weights = jnp.stack([w_in.T, w_out])
    weights = jnp.concatenate([weights, swap(weights, "chan", 2)], axis=1)
    weights = jnp.concatenate([weights, swap(weights, "chan", 1)], axis=1)
    rimmed_image = extended(image, (("rows", 2),), 3)
    padded = jnp.pad(rimmed_image.astype(f32), ((0, 0), (0, 0), (0, 0), (3, 3)))
    mixed_in = forward_taps(padded, dw_kernel, height, breadth).astype(bf16)
    mixed_flat = mixed_in.reshape(channels, pixels)
    cotan_flat = cotangent.reshape(channels, pixels).astype(f32)
    scaled = (layer_scale[:, None] * cotan_flat).astype(bf16)
    gain_row = jnp.pad(ln_gain[None, :], ((0, 0), (0, 128 - channels)))
    mixed_all, scaled_all, gain_all = exchange(
        spread_kernel,
        0,
        (mixed_flat, scaled, gain_row),
        ((n, channels, part), (n, channels, part), (n, 1, 128)),
        n,
        part,
    )
    mixed_all = mixed_all.reshape(n * channels, part).astype(f32)
    scaled_all = scaled_all.reshape(n * channels, part)
    gain_all = gain_all[:, 0, :channels].reshape(n * channels, 1)
    centre = jnp.mean(mixed_all, axis=0)
    spread = jnp.mean(jnp.square(mixed_all - centre), axis=0)
    inv_scale = lax.rsqrt(spread + epsilon)
    unit_all = (mixed_all - centre) * inv_scale
    normed = (unit_all * gain_all).astype(bf16)
    pre_act = jnp.dot(weights[0], normed, preferred_element_type=f32)
    grad_act = jnp.dot(weights[1], scaled_all, preferred_element_type=f32)
    activated = jax.nn.gelu(pre_act, approximate=False).astype(bf16)
    grad_pre = (grad_act * gelu_slope(pre_act)).astype(bf16)
    branch_part = lax.dot_general(
        weights[1], activated, contract_lead, preferred_element_type=f32
    ).astype(bf16)
    normed_part = lax.dot_general(weights[0], grad_pre, contract_lead, preferred_element_type=f32)
    gained_part = normed_part * gain_all
    stats = jnp.stack(
        [jnp.sum(gained_part, axis=0), jnp.sum(gained_part * unit_all, axis=0), centre, inv_scale]
    )
    grad_w_in = lax.dot_general(grad_pre, normed, contract_tail, preferred_element_type=f32)
    grad_w_out = lax.dot_general(activated, scaled_all, contract_tail, preferred_element_type=f32)
    branch_all, normed_all, stats_all = exchange(
        collect_kernel,
        1,
        (
            branch_part.reshape(n, channels, part),
            normed_part.astype(bf16).reshape(n, channels, part),
            stats,
        ),
        ((planes, channels, pixels), (planes, channels, pixels), (planes, 4, pixels)),
        n,
        part,
    )
    grads = jnp.stack([grad_w_in, grad_w_out])
    for bit in (1, 2):
        half = grads.shape[1] // 2
        grads = grads[:, :half] + swap(grads[:, half:].astype(bf16), "chan", bit).astype(f32)
    grads = total_over(grads, "rows")
    branch = jnp.sum(branch_all.astype(f32), axis=0)
    grad_normed = jnp.sum(normed_all.astype(f32), axis=0)
    total_one = jnp.sum(stats_all[:, 0], axis=0)
    total_two = jnp.sum(stats_all[:, 1], axis=0)
    centre, inv_scale = stats_all[0, 2], stats_all[0, 3]
    image_flat = image.reshape(channels, pixels).astype(f32)
    block_out = (image_flat + layer_scale[:, None] * branch).astype(bf16).reshape(image.shape)
    grad_scale = jnp.sum(cotan_flat * branch, axis=1)
    unit_norm = (mixed_flat.astype(f32) - centre) * inv_scale
    grad_gain = jnp.sum(grad_normed * unit_norm, axis=1)
    scaled_grad = grad_normed * ln_gain[:, None]
    grad_mixed = (inv_scale * (scaled_grad - total_one / D - unit_norm * (total_two / D))).astype(
        bf16
    )
    grad_mixed = grad_mixed.reshape(channels, images, height, breadth)
    rimmed_grad = extended(grad_mixed, (("rows", 2),), 3)
    rimmed_grad = jnp.pad(rimmed_grad.astype(f32), ((0, 0), (0, 0), (0, 0), (3, 3)))
    spread_back = transpose_taps(rimmed_grad, dw_kernel, height, breadth)
    grad_image = (cotangent.astype(f32) + spread_back).astype(bf16)
    grad_kernel = correlate_taps(padded, grad_mixed.astype(f32), height, breadth)
    small = jnp.concatenate(
        [grad_kernel.reshape(channels, KSIZE * KSIZE), grad_gain[:, None], grad_scale[:, None]],
        axis=1,
    )
    small = total_over(small, "rows")
    grad_kernel = small[:, : KSIZE * KSIZE].reshape(channels, KSIZE, KSIZE)
    return (
        block_out,
        grad_image,
        grad_kernel,
        small[:, KSIZE * KSIZE],
        small[:, KSIZE * KSIZE + 1],
        grads[0].T,
        grads[1],
    )


def solution(mesh):
    return jax.shard_map(
        body,
        mesh=mesh,
        in_specs=(
            P("chan", None, "rows", None),
            P("chan", None, None),
            P("chan"),
            P(None, "chan"),
            P("chan", None),
            P("chan"),
            P("chan", None, "rows", None),
        ),
        out_specs=(
            P("chan", None, "rows", None),
            P("chan", None, "rows", None),
            P("chan", None, None),
            P("chan"),
            P("chan"),
            P(None, "chan"),
            P("chan", None),
        ),
        check_vma=False,
    )
```

```python
import functools

import jax
import jax.numpy as jnp
from jax import lax
from jax.experimental import pallas as pl
from jax.experimental.pallas import tpu as pltpu
from jax.sharding import PartitionSpec as P

D = 768
KSIZE = 7


epsilon = 1e-06
inv_root_two = 0.7071067811865476
inv_root_two_pi = 0.3989422804014327


def extended(block, axis):
    count = lax.axis_size(axis)
    forward = [(i, i + 1) for i in range(count - 1)]
    backward = [(target, source) for source, target in forward]
    low = lax.ppermute(block[-3:], axis, forward)
    high = lax.ppermute(block[:3], axis, backward)
    return jnp.concatenate([low, block, high], axis=0)


def gelu_slope(values):
    return (
        0.5 * (1.0 + lax.erf(values * inv_root_two))
        + values * jnp.exp(-0.5 * values * values) * inv_root_two_pi
    )


GROUP = 4
MESH = pl.DeviceIdType.MESH


def greet(n, me):
    barrier = pltpu.get_barrier_semaphore()
    for k in range(1, n):
        pl.semaphore_signal(
            barrier, inc=1, device_id={"chan": lax.rem(me + k, n)}, device_id_type=MESH
        )
    pl.semaphore_wait(barrier, n - 1)


def spread_kernel(n, part, *refs):
    count = (len(refs) - 3) // 2
    sources, targets = refs[:count], refs[count : 2 * count]
    local_sem, send_sem, recv_sem = refs[2 * count :]
    me = lax.axis_index("chan")
    greet(n, me)

    def piece(ref, peer):
        if ref.shape[0] == part * GROUP:
            return ref.at[pl.ds(lax.rem(peer, GROUP) * part, part)]
        return ref

    copies = []
    for k in range(1, n):
        peer = lax.rem(me + k, n)
        for a in range(count):
            copy = pltpu.make_async_remote_copy(
                src_ref=piece(sources[a], peer),
                dst_ref=targets[a].at[:, me],
                send_sem=send_sem.at[a, k],
                recv_sem=recv_sem.at[a, k],
                device_id={"chan": peer},
                device_id_type=MESH,
            )
            copy.start()
            copies.append(copy)
    own = []
    for a in range(count):
        copy = pltpu.make_async_copy(piece(sources[a], me), targets[a].at[:, me], local_sem.at[a])
        copy.start()
        own.append(copy)
    for copy in own + copies:
        copy.wait()


def collect_kernel(n, part, *refs):
    count = (len(refs) - 3) // 2
    sources, targets = refs[:count], refs[count : 2 * count]
    local_sem, send_sem, recv_sem = refs[2 * count :]
    me = lax.axis_index("chan")
    plane = lax.div(me, GROUP)
    greet(n, me)
    lines = pl.ds(lax.rem(me, GROUP) * part, part)

    def piece(ref, peer):
        return ref.at[:, peer] if len(ref.shape) == 4 else ref

    copies = []
    for k in range(1, n):
        peer = lax.rem(me + k, n)
        for a in range(count):
            copy = pltpu.make_async_remote_copy(
                src_ref=piece(sources[a], peer),
                dst_ref=targets[a].at[plane, lines],
                send_sem=send_sem.at[a, k],
                recv_sem=recv_sem.at[a, k],
                device_id={"chan": peer},
                device_id_type=MESH,
            )
            copy.start()
            copies.append(copy)
    own = []
    for a in range(count):
        copy = pltpu.make_async_copy(
            piece(sources[a], me), targets[a].at[plane, lines], local_sem.at[a]
        )
        copy.start()
        own.append(copy)
    for copy in own + copies:
        copy.wait()


def exchange(kernel, identity, arrays, shapes, n, part):
    count = len(arrays)
    size = sum(a.size * a.dtype.itemsize for a in arrays)
    return pl.pallas_call(
        functools.partial(kernel, n, part),
        out_shape=tuple(
            jax.ShapeDtypeStruct(shape, a.dtype) for shape, a in zip(shapes, arrays)
        ),
        in_specs=[pl.BlockSpec(memory_space=pl.ANY)] * count,
        out_specs=tuple([pl.BlockSpec(memory_space=pl.ANY)] * count),
        scratch_shapes=[
            pltpu.SemaphoreType.DMA((count,)),
            pltpu.SemaphoreType.DMA((count, n)),
            pltpu.SemaphoreType.DMA((count, n)),
        ],
        compiler_params=pltpu.CompilerParams(collective_id=identity, has_side_effects=True),
        cost_estimate=pl.CostEstimate(flops=0, bytes_accessed=100 * size, transcendentals=0),
    )(*arrays)


def swap(value, axis, bit):
    n = lax.axis_size(axis)
    return lax.ppermute(value, axis, [(i, i ^ bit) for i in range(n)])


def total_over(value, axis):
    bit = 1
    while bit < lax.axis_size(axis):
        near = value.astype(jnp.bfloat16)
        value = near.astype(jnp.float32) + swap(near, axis, bit).astype(jnp.float32)
        bit *= 2
    return value


def shifted(value, shift):
    if shift == 0:
        return value
    breadth = value.shape[1]
    lane = lax.broadcasted_iota(jnp.int32, value.shape, 1)
    rolled = pltpu.roll(value, shift % breadth, 1)
    keep = lane >= shift if shift > 0 else lane < breadth + shift
    return jnp.where(keep, rolled, 0.0)


def forward_kernel(padded_ref, taps_ref, mixed_ref):
    height = mixed_ref.shape[0]
    taps = taps_ref[...]
    sums = [None] * height
    for v in range(KSIZE):
        lines = [shifted(padded_ref[r], 3 - v) for r in range(height + 6)]
        for u in range(KSIZE):
            t = u * KSIZE + v
            tap = jnp.broadcast_to(taps[:, t : t + 1], lines[0].shape)
            for r in range(height):
                term = tap * lines[r + u]
                sums[r] = term if sums[r] is None else sums[r] + term
    for r in range(height):
        mixed_ref[r] = sums[r].astype(mixed_ref.dtype)


def backward_kernel(grad_ref, padded_ref, taps_ref, cotan_ref, image_grad_ref, taps_grad_ref):
    height = cotan_ref.shape[0]
    taps = taps_ref[...]
    lane = lax.broadcasted_iota(jnp.int32, taps.shape, 1)
    taps_grad = jnp.zeros_like(taps)
    sums = [None] * height
    for v in range(KSIZE):
        lines = [shifted(grad_ref[r], v - 3) for r in range(height + 6)]
        for u in range(KSIZE):
            t = u * KSIZE + v
            tap = jnp.broadcast_to(taps[:, t : t + 1], lines[0].shape)
            for r in range(height):
                term = tap * lines[r + 6 - u]
                sums[r] = term if sums[r] is None else sums[r] + term
            both = [lines[r + 3] * padded_ref[r + u] for r in range(height)]
            while len(both) > 1:
                both = [p + q for p, q in zip(both[::2], both[1::2])] + both[len(both) // 2 * 2 :]
            taps_grad = jnp.where(lane == t, jnp.sum(both[0], axis=1, keepdims=True), taps_grad)
    for r in range(height):
        image_grad_ref[r] = (sums[r] + cotan_ref[r].astype(jnp.float32)).astype(
            image_grad_ref.dtype
        )
    taps_grad_ref[...] = taps_grad


def stencil(kernel, arrays, outs):
    channels = arrays[0].shape[1]

    def spec(value):
        if len(value.shape) == 2:
            return pl.BlockSpec((8, value.shape[1]), lambda i: (i, 0))
        return pl.BlockSpec((value.shape[0], 8, value.shape[2]), lambda i: (0, i, 0))

    return pl.pallas_call(
        kernel,
        grid=(channels // 8,),
        out_shape=tuple(outs),
        in_specs=[spec(a) for a in arrays],
        out_specs=tuple(spec(o) for o in outs),
        cost_estimate=pl.CostEstimate(
            flops=10000000, bytes_accessed=6000000, transcendentals=0
        ),
    )(*arrays)


def body(image, dw_kernel, ln_gain, w_in, w_out, layer_scale, cotangent):
    channels, images, height, breadth = image.shape
    part = height // GROUP
    n = lax.axis_size("chan")
    every = n * channels
    planes = n // GROUP
    contract_lead = (((0,), (0,)), ((), ()))
    contract_tail = (((1,), (1,)), ((), ()))
    bf16, f32 = jnp.bfloat16, jnp.float32
    image_rows = jnp.transpose(image[:, 0], (1, 0, 2))
    cotan_rows = jnp.transpose(cotangent[:, 0], (1, 0, 2))
    taps = jnp.pad(dw_kernel.reshape(channels, KSIZE * KSIZE), ((0, 0), (0, 128 - KSIZE * KSIZE)))
    padded = extended(image_rows, "rows").astype(f32)
    weights = jnp.stack([w_in.T, w_out])
    weights = jnp.concatenate([weights, swap(weights, "chan", 2)], axis=1)
    weights = jnp.concatenate([weights, swap(weights, "chan", 1)], axis=1)
    (mixed_in,) = stencil(
        forward_kernel, (padded, taps), (jax.ShapeDtypeStruct(image_rows.shape, bf16),)
    )
    scaled = (layer_scale[:, None] * cotan_rows.astype(f32)).astype(bf16)
    gain_row = jnp.pad(ln_gain[None, None, :], ((0, 0), (0, 0), (0, 128 - channels)))
    mixed_all, scaled_all, gain_all = exchange(
        spread_kernel,
        0,
        (mixed_in, scaled, gain_row),
        ((part, n, channels, breadth), (part, n, channels, breadth), (1, n, 1, 128)),
        n,
        part,
    )

    def flat(value):
        value = value.reshape(part, every, breadth)
        return jnp.concatenate([value[i] for i in range(part)], axis=1)

    def split(value):
        value = jnp.stack([value[:, i * breadth : (i + 1) * breadth] for i in range(part)])
        return value.reshape(part, n, channels, breadth)

    mixed_all = flat(mixed_all).astype(f32)
    scaled_all = flat(scaled_all)
    gain_all = gain_all[0, :, 0, :channels].reshape(every, 1)
    centre = jnp.mean(mixed_all, axis=0)
    spread = jnp.mean(jnp.square(mixed_all - centre), axis=0)
    inv_scale = lax.rsqrt(spread + epsilon)
    unit_all = (mixed_all - centre) * inv_scale
    normed = (unit_all * gain_all).astype(bf16)
    pre_act = jnp.dot(weights[0], normed, preferred_element_type=f32)
    grad_act = jnp.dot(weights[1], scaled_all, preferred_element_type=f32)
    activated = jax.nn.gelu(pre_act, approximate=False).astype(bf16)
    grad_pre = (grad_act * gelu_slope(pre_act)).astype(bf16)
    branch_part = lax.dot_general(
        weights[1], activated, contract_lead, preferred_element_type=f32
    ).astype(bf16)
    normed_part = lax.dot_general(weights[0], grad_pre, contract_lead, preferred_element_type=f32)
    gained_part = normed_part * gain_all
    stats = jnp.stack(
        [jnp.sum(gained_part, axis=0), jnp.sum(gained_part * unit_all, axis=0), centre, inv_scale]
    )
    stats = jnp.transpose(stats.reshape(4, part, breadth), (1, 0, 2))
    grad_w_in = lax.dot_general(grad_pre, normed, contract_tail, preferred_element_type=f32)
    grad_w_out = lax.dot_general(activated, scaled_all, contract_tail, preferred_element_type=f32)
    branch_all, normed_all, stats_all = exchange(
        collect_kernel,
        1,
        (split(branch_part), split(normed_part.astype(bf16)), stats),
        (
            (planes, height, channels, breadth),
            (planes, height, channels, breadth),
            (planes, height, 4, breadth),
        ),
        n,
        part,
    )
    grads = jnp.stack([grad_w_in, grad_w_out])
    for bit in (1, 2):
        half = grads.shape[1] // 2
        grads = grads[:, :half] + swap(grads[:, half:].astype(bf16), "chan", bit).astype(f32)
    grads = total_over(grads, "rows")
    branch = jnp.sum(branch_all.astype(f32), axis=0)
    grad_normed = jnp.sum(normed_all.astype(f32), axis=0)
    total_one = jnp.sum(stats_all[:, :, 0:1], axis=0)
    total_two = jnp.sum(stats_all[:, :, 1:2], axis=0)
    centre, inv_scale = stats_all[0, :, 2:3], stats_all[0, :, 3:4]
    unit_norm = (mixed_in.astype(f32) - centre) * inv_scale
    scaled_grad = grad_normed * ln_gain[:, None]
    grad_mixed = (inv_scale * (scaled_grad - total_one / D - unit_norm * (total_two / D))).astype(
        bf16
    )
    rimmed_grad = extended(grad_mixed, "rows").astype(f32)
    image_grad, grad_kernel = stencil(
        backward_kernel,
        (rimmed_grad, padded, taps, cotan_rows),
        (
            jax.ShapeDtypeStruct(image_rows.shape, bf16),
            jax.ShapeDtypeStruct((channels, 128), f32),
        ),
    )
    block_out = (image_rows.astype(f32) + layer_scale[:, None] * branch).astype(bf16)
    grad_scale = jnp.sum(cotan_rows.astype(f32) * branch, axis=(0, 2))
    grad_gain = jnp.sum(grad_normed * unit_norm, axis=(0, 2))
    small = jnp.concatenate(
        [grad_kernel[:, : KSIZE * KSIZE], grad_gain[:, None], grad_scale[:, None]], axis=1
    )
    small = total_over(small, "rows")
    grad_kernel = small[:, : KSIZE * KSIZE].reshape(channels, KSIZE, KSIZE)
    return (
        jnp.transpose(block_out, (1, 0, 2))[:, None],
        jnp.transpose(image_grad, (1, 0, 2))[:, None],
        grad_kernel,
        small[:, KSIZE * KSIZE],
        small[:, KSIZE * KSIZE + 1],
        grads[0].T,
        grads[1],
    )


def solution(mesh):
    return jax.shard_map(
        body,
        mesh=mesh,
        in_specs=(
            P("chan", None, "rows", None),
            P("chan", None, None),
            P("chan"),
            P(None, "chan"),
            P("chan", None),
            P("chan"),
            P("chan", None, "rows", None),
        ),
        out_specs=(
            P("chan", None, "rows", None),
            P("chan", None, "rows", None),
            P("chan", None, None),
            P("chan"),
            P("chan"),
            P(None, "chan"),
            P("chan", None),
        ),
        check_vma=False,
    )
```

```python
import functools

import jax
import jax.numpy as jnp
from jax import lax
from jax.experimental import pallas as pl
from jax.experimental.pallas import tpu as pltpu
from jax.sharding import PartitionSpec as P

D = 768
KSIZE = 7


epsilon = 1e-06
inv_root_two = 0.7071067811865476
inv_root_two_pi = 0.3989422804014327


def extended(block, axis):
    count = lax.axis_size(axis)
    forward = [(i, i + 1) for i in range(count - 1)]
    backward = [(target, source) for source, target in forward]
    low = lax.ppermute(block[-3:], axis, forward)
    high = lax.ppermute(block[:3], axis, backward)
    return jnp.concatenate([low, block, high], axis=0)


def gelu_slope(values):
    return (
        0.5 * (1.0 + lax.erf(values * inv_root_two))
        + values * jnp.exp(-0.5 * values * values) * inv_root_two_pi
    )


GROUP = 4
MESH = pl.DeviceIdType.MESH


def greet(n, me):
    barrier = pltpu.get_barrier_semaphore()
    for k in range(1, n):
        pl.semaphore_signal(
            barrier, inc=1, device_id={"chan": lax.rem(me + k, n)}, device_id_type=MESH
        )
    pl.semaphore_wait(barrier, n - 1)


def spread_kernel(n, part, *refs):
    count = (len(refs) - 3) // 2
    sources, targets = refs[:count], refs[count : 2 * count]
    local_sem, send_sem, recv_sem = refs[2 * count :]
    me = lax.axis_index("chan")
    greet(n, me)

    def piece(ref, peer):
        if ref.shape[0] == part * GROUP:
            return ref.at[pl.ds(lax.rem(peer, GROUP) * part, part)]
        return ref

    copies = []
    for k in range(1, n):
        peer = lax.rem(me + k, n)
        for a in range(count):
            copy = pltpu.make_async_remote_copy(
                src_ref=piece(sources[a], peer),
                dst_ref=targets[a].at[:, me],
                send_sem=send_sem.at[a, k],
                recv_sem=recv_sem.at[a, k],
                device_id={"chan": peer},
                device_id_type=MESH,
            )
            copy.start()
            copies.append(copy)
    own = []
    for a in range(count):
        copy = pltpu.make_async_copy(piece(sources[a], me), targets[a].at[:, me], local_sem.at[a])
        copy.start()
        own.append(copy)
    for copy in own + copies:
        copy.wait()


def exchange(kernel, identity, arrays, shapes, n, part):
    count = len(arrays)
    size = sum(a.size * a.dtype.itemsize for a in arrays)
    return pl.pallas_call(
        functools.partial(kernel, n, part),
        out_shape=tuple(
            jax.ShapeDtypeStruct(shape, a.dtype) for shape, a in zip(shapes, arrays)
        ),
        in_specs=[pl.BlockSpec(memory_space=pl.ANY)] * count,
        out_specs=tuple([pl.BlockSpec(memory_space=pl.ANY)] * count),
        scratch_shapes=[
            pltpu.SemaphoreType.DMA((count,)),
            pltpu.SemaphoreType.DMA((count, n)),
            pltpu.SemaphoreType.DMA((count, n)),
        ],
        compiler_params=pltpu.CompilerParams(collective_id=identity, has_side_effects=True),
        cost_estimate=pl.CostEstimate(flops=0, bytes_accessed=100 * size, transcendentals=0),
    )(*arrays)


def swap(value, axis, bit):
    n = lax.axis_size(axis)
    return lax.ppermute(value, axis, [(i, i ^ bit) for i in range(n)])


def shifted(value, shift):
    if shift == 0:
        return value
    breadth = value.shape[1]
    lane = lax.broadcasted_iota(jnp.int32, value.shape, 1)
    rolled = pltpu.roll(value, shift % breadth, 1)
    keep = lane >= shift if shift > 0 else lane < breadth + shift
    return jnp.where(keep, rolled, 0.0)


def forward_kernel(padded_ref, taps_ref, mixed_ref):
    height = mixed_ref.shape[0]
    taps = taps_ref[...]
    sums = [None] * height
    for v in range(KSIZE):
        lines = [shifted(padded_ref[r], 3 - v) for r in range(height + 6)]
        for u in range(KSIZE):
            t = u * KSIZE + v
            tap = jnp.broadcast_to(taps[:, t : t + 1], lines[0].shape)
            for r in range(height):
                term = tap * lines[r + u]
                sums[r] = term if sums[r] is None else sums[r] + term
    for r in range(height):
        mixed_ref[r] = sums[r].astype(mixed_ref.dtype)


def flipped(index, bit):
    return index + bit - 2 * bit * lax.rem(lax.div(index, bit), 2)


def finish_kernel(
    n,
    rows,
    part,
    branch_ref,
    normed_ref,
    stats_ref,
    sent_ref,
    kept_ref,
    mixed_ref,
    padded_ref,
    image_ref,
    cotan_ref,
    taps_ref,
    gain_ref,
    scale_ref,
    block_ref,
    image_grad_ref,
    small_ref,
    grads_ref,
    branch_in,
    normed_in,
    stats_in,
    core_in,
    near_out,
    near_in,
    row_out,
    row_in,
    grad_pad,
    running,
    sums_one,
    sums_two,
    halo_out,
    halo_in,
    small_out,
    small_in,
    local_sem,
    send_sem,
    recv_sem,
    pair_send,
    pair_recv,
):
    f32, bf16 = jnp.float32, jnp.bfloat16
    me = lax.axis_index("chan")
    row = lax.axis_index("rows")
    plane = lax.div(me, GROUP)
    lines = pl.ds(lax.rem(me, GROUP) * part, part)
    height, channels, breadth = mixed_ref.shape
    planes = n // GROUP
    steps = row_out.shape[0]
    hidden = grads_ref.shape[1]
    up, down = lax.rem(row + rows - 1, rows), lax.rem(row + 1, rows)
    partners = [flipped(row, 2**s) for s in range(steps)]

    barrier = pltpu.get_barrier_semaphore()
    for k in range(1, n):
        pl.semaphore_signal(
            barrier, inc=1, device_id={"chan": lax.rem(me + k, n)}, device_id_type=MESH
        )
    for other in [up, down] + partners:
        pl.semaphore_signal(barrier, inc=1, device_id={"rows": other}, device_id_type=MESH)
    pl.semaphore_wait(barrier, n + 1 + steps)

    def pair(index, source, target, device):
        copy = pltpu.make_async_remote_copy(
            src_ref=source,
            dst_ref=target,
            send_sem=pair_send.at[index],
            recv_sem=pair_recv.at[index],
            device_id=device,
            device_id_type=MESH,
        )
        copy.start()
        return copy

    def scatter(a, piece, target):
        copies = []
        for k in range(1, n):
            peer = lax.rem(me + k, n)
            copy = pltpu.make_async_remote_copy(
                src_ref=piece(peer),
                dst_ref=target.at[plane, lines],
                send_sem=send_sem.at[a, k],
                recv_sem=recv_sem.at[a, k],
                device_id={"chan": peer},
                device_id_type=MESH,
            )
            copy.start()
            copies.append(copy)
        copy = pltpu.make_async_copy(piece(me), target.at[plane, lines], local_sem.at[a])
        copy.start()
        return copies + [copy]

    first = scatter(0, lambda peer: stats_ref, stats_in)
    first += scatter(1, lambda peer: normed_ref.at[:, peer], normed_in)
    core = pair(0, sent_ref, core_in, {"chan": flipped(me, 1)})
    core.wait()

    @pl.loop(0, hidden // 16)
    def _(i):
        for a in range(2):
            own = pl.ds(pl.multiple_of(16 * i, 16), 16)
            other = pl.ds(pl.multiple_of(hidden + 16 * i, 16), 16)
            grads_ref[a, own, :] = kept_ref[a, own, :] + core_in[a, own, :].astype(f32)
            near_out[a, own, :] = (
                kept_ref[a, other, :] + core_in[a, other, :].astype(f32)
            ).astype(bf16)

    near = pair(1, near_out, near_in, {"chan": flipped(me, 2)})
    for copy in first:
        copy.wait()
    last = scatter(2, lambda peer: branch_ref.at[:, peer], branch_in)

    sums_one[...] = jnp.zeros_like(sums_one)
    sums_two[...] = jnp.zeros_like(sums_two)

    def normalize(start, stop):
        @pl.loop(start, stop)
        def _(r):
            grad_normed = normed_in[0, r].astype(f32)
            stats = stats_in[0, r]
            centre, inv_scale = stats[2:3], stats[3:4]
            for p in range(1, planes):
                grad_normed += normed_in[p, r].astype(f32)
                stats += stats_in[p, r]
            unit = (mixed_ref[r].astype(f32) - centre) * inv_scale
            sums_one[...] += grad_normed * unit
            scaled_grad = grad_normed * gain_ref[...]
            mixed_grad = inv_scale * (
                scaled_grad - stats[0:1] * (1.0 / D) - unit * (stats[1:2] * (1.0 / D))
            )
            grad_pad[r + 3] = mixed_grad.astype(bf16).astype(f32)

    normalize(0, 3)
    normalize(height - 3, height)
    for i in range(3):
        halo_out[0, i] = grad_pad[3 + i].astype(bf16)
        halo_out[1, i] = grad_pad[height + i].astype(bf16)
    halos = [
        pair(2, halo_out.at[0], halo_in.at[1], {"rows": up}),
        pair(3, halo_out.at[1], halo_in.at[0], {"rows": down}),
    ]
    normalize(3, height - 3)
    near.wait()

    @pl.loop(0, hidden // 16)
    def _(i):
        for a in range(2):
            own = pl.ds(pl.multiple_of(16 * i, 16), 16)
            row_out[0, a, own, :] = (grads_ref[a, own, :] + near_in[a, own, :].astype(f32)).astype(
                bf16
            )

    step = pair(4, row_out.at[0], row_in.at[0], {"rows": partners[0]})
    for copy in halos:
        copy.wait()
    above = jnp.where(row > 0, 1.0, 0.0).astype(f32)
    below = jnp.where(row < rows - 1, 1.0, 0.0).astype(f32)
    for i in range(3):
        grad_pad[i] = halo_in[0, i].astype(f32) * above
        grad_pad[height + 3 + i] = halo_in[1, i].astype(f32) * below

    @pl.loop(0, channels // 8)
    def _(g):
        group = pl.ds(pl.multiple_of(8 * g, 8), 8)
        taps = taps_ref[group, :]
        lane = lax.broadcasted_iota(jnp.int32, taps.shape, 1)
        taps_grad = jnp.zeros_like(taps)
        sums = [None] * height
        for v in range(KSIZE):
            shifts = [shifted(grad_pad[r, group, :], v - 3) for r in range(height + 6)]
            for u in range(KSIZE):
                t = u * KSIZE + v
                tap = jnp.broadcast_to(taps[:, t : t + 1], taps.shape)
                for r in range(height):
                    term = tap * shifts[r + 6 - u]
                    sums[r] = term if sums[r] is None else sums[r] + term
                both = [shifts[r + 3] * padded_ref[r + u, group, :] for r in range(height)]
                while len(both) > 1:
                    both = [p + q for p, q in zip(both[::2], both[1::2])] + both[
                        len(both) // 2 * 2 :
                    ]
                taps_grad = jnp.where(
                    lane == t, jnp.sum(both[0], axis=1, keepdims=True), taps_grad
                )
        for r in range(height):
            running[r, group, :] = sums[r]
        small_ref[group, :] = taps_grad

    @pl.loop(0, height)
    def _(r):
        image_grad_ref[r] = (running[r] + cotan_ref[r].astype(f32)).astype(bf16)

    for s in range(steps):
        step.wait()
        final = s == steps - 1

        @pl.loop(0, hidden // 16)
        def _(i):
            for a in range(2):
                own = pl.ds(pl.multiple_of(16 * i, 16), 16)
                total = row_out[s, a, own, :].astype(f32) + row_in[s, a, own, :].astype(f32)
                if final:
                    grads_ref[a, own, :] = total
                else:
                    row_out[s + 1, a, own, :] = total.astype(bf16)

        if not final:
            step = pair(
                5 + s, row_out.at[s + 1], row_in.at[s + 1], {"rows": partners[s + 1]}
            )
    for copy in last:
        copy.wait()

    @pl.loop(0, height)
    def _(r):
        branch = branch_in[0, r].astype(f32)
        for p in range(1, planes):
            branch += branch_in[p, r].astype(f32)
        sums_two[...] += branch * cotan_ref[r].astype(f32)
        block_ref[r] = (image_ref[r].astype(f32) + scale_ref[...] * branch).astype(bf16)

    lane = lax.broadcasted_iota(jnp.int32, small_ref.shape, 1)
    small = small_ref[...]
    small = jnp.where(lane == KSIZE * KSIZE, jnp.sum(sums_one[...], axis=1, keepdims=True), small)
    small = jnp.where(
        lane == KSIZE * KSIZE + 1, jnp.sum(sums_two[...], axis=1, keepdims=True), small
    )
    for s in range(steps):
        small_out[s] = small
        step = pair(4 + steps + s, small_out.at[s], small_in.at[s], {"rows": partners[s]})
        step.wait()
        small = small + small_in[s]
    small_ref[...] = small


def finish(n, part, arrays, hidden):
    f32, bf16 = jnp.float32, jnp.bfloat16
    height, channels, breadth = arrays[5].shape
    width = arrays[3].shape[2]
    planes = n // GROUP
    rows = lax.axis_size("rows")
    steps = rows.bit_length() - 1
    pairs = 4 + 2 * steps
    vmem = pl.BlockSpec(memory_space=pltpu.VMEM)
    hbm = pl.BlockSpec(memory_space=pl.ANY)
    dma = pltpu.SemaphoreType.DMA
    return pl.pallas_call(
        functools.partial(finish_kernel, n, rows, part),
        out_shape=(
            jax.ShapeDtypeStruct((height, channels, breadth), bf16),
            jax.ShapeDtypeStruct((height, channels, breadth), bf16),
            jax.ShapeDtypeStruct((channels, 128), f32),
            jax.ShapeDtypeStruct((2, hidden, width), f32),
        ),
        in_specs=[hbm] * 4 + [vmem] * 8,
        out_specs=(vmem, vmem, vmem, vmem),
        scratch_shapes=[
            pltpu.VMEM((planes, height, channels, breadth), bf16),
            pltpu.VMEM((planes, height, channels, breadth), bf16),
            pltpu.VMEM((planes, height, 4, breadth), f32),
            pltpu.VMEM((2, 2 * hidden, width), bf16),
            pltpu.VMEM((2, hidden, width), bf16),
            pltpu.VMEM((2, hidden, width), bf16),
            pltpu.VMEM((steps, 2, hidden, width), bf16),
            pltpu.VMEM((steps, 2, hidden, width), bf16),
            pltpu.VMEM((height + 6, channels, breadth), f32),
            pltpu.VMEM((height, channels, breadth), f32),
            pltpu.VMEM((channels, breadth), f32),
            pltpu.VMEM((channels, breadth), f32),
            pltpu.VMEM((2, 3, channels, breadth), bf16),
            pltpu.VMEM((2, 3, channels, breadth), bf16),
            pltpu.VMEM((steps, channels, 128), f32),
            pltpu.VMEM((steps, channels, 128), f32),
            dma((3,)),
            dma((3, n)),
            dma((3, n)),
            dma((pairs,)),
            dma((pairs,)),
        ],
        compiler_params=pltpu.CompilerParams(
            collective_id=1, has_side_effects=True, vmem_limit_bytes=36 * 2**20
        ),
        cost_estimate=pl.CostEstimate(
            flops=40000000, bytes_accessed=100000000, transcendentals=0
        ),
    )(*arrays)


def stencil(kernel, arrays, outs):
    channels = arrays[0].shape[1]

    def spec(value):
        if len(value.shape) == 2:
            return pl.BlockSpec((8, value.shape[1]), lambda i: (i, 0))
        return pl.BlockSpec((value.shape[0], 8, value.shape[2]), lambda i: (0, i, 0))

    return pl.pallas_call(
        kernel,
        grid=(channels // 8,),
        out_shape=tuple(outs),
        in_specs=[spec(a) for a in arrays],
        out_specs=tuple(spec(o) for o in outs),
        cost_estimate=pl.CostEstimate(
            flops=10000000, bytes_accessed=6000000, transcendentals=0
        ),
    )(*arrays)


def body(image, dw_kernel, ln_gain, w_in, w_out, layer_scale, cotangent):
    channels, images, height, breadth = image.shape
    part = height // GROUP
    n = lax.axis_size("chan")
    every = n * channels
    planes = n // GROUP
    contract_lead = (((0,), (0,)), ((), ()))
    contract_tail = (((1,), (1,)), ((), ()))
    bf16, f32 = jnp.bfloat16, jnp.float32
    image_rows = jnp.transpose(image[:, 0], (1, 0, 2))
    cotan_rows = jnp.transpose(cotangent[:, 0], (1, 0, 2))
    taps = jnp.pad(dw_kernel.reshape(channels, KSIZE * KSIZE), ((0, 0), (0, 128 - KSIZE * KSIZE)))
    padded = extended(image_rows, "rows").astype(f32)
    weights = jnp.stack([w_in.T, w_out])
    weights = jnp.concatenate([weights, swap(weights, "chan", 2)], axis=1)
    weights = jnp.concatenate([weights, swap(weights, "chan", 1)], axis=1)
    (mixed_in,) = stencil(
        forward_kernel, (padded, taps), (jax.ShapeDtypeStruct(image_rows.shape, bf16),)
    )
    scaled = (layer_scale[:, None] * cotan_rows.astype(f32)).astype(bf16)
    gain_row = jnp.pad(ln_gain[None, None, :], ((0, 0), (0, 0), (0, 128 - channels)))
    mixed_all, scaled_all, gain_all = exchange(
        spread_kernel,
        0,
        (mixed_in, scaled, gain_row),
        ((part, n, channels, breadth), (part, n, channels, breadth), (1, n, 1, 128)),
        n,
        part,
    )

    def flat(value):
        value = value.reshape(part, every, breadth)
        return jnp.concatenate([value[i] for i in range(part)], axis=1)

    def split(value):
        value = jnp.stack([value[:, i * breadth : (i + 1) * breadth] for i in range(part)])
        return value.reshape(part, n, channels, breadth)

    mixed_all = flat(mixed_all).astype(f32)
    scaled_all = flat(scaled_all)
    gain_all = gain_all[0, :, 0, :channels].reshape(every, 1)
    centre = jnp.mean(mixed_all, axis=0)
    spread = jnp.mean(jnp.square(mixed_all - centre), axis=0)
    inv_scale = lax.rsqrt(spread + epsilon)
    unit_all = (mixed_all - centre) * inv_scale
    normed = (unit_all * gain_all).astype(bf16)
    pre_act = jnp.dot(weights[0], normed, preferred_element_type=f32)
    grad_act = jnp.dot(weights[1], scaled_all, preferred_element_type=f32)
    activated = jax.nn.gelu(pre_act, approximate=False).astype(bf16)
    grad_pre = (grad_act * gelu_slope(pre_act)).astype(bf16)
    branch_part = lax.dot_general(
        weights[1], activated, contract_lead, preferred_element_type=f32
    ).astype(bf16)
    normed_part = lax.dot_general(weights[0], grad_pre, contract_lead, preferred_element_type=f32)
    gained_part = normed_part * gain_all
    stats = jnp.stack(
        [jnp.sum(gained_part, axis=0), jnp.sum(gained_part * unit_all, axis=0), centre, inv_scale]
    )
    stats = jnp.transpose(stats.reshape(4, part, breadth), (1, 0, 2))
    grad_w_in = lax.dot_general(grad_pre, normed, contract_tail, preferred_element_type=f32)
    grad_w_out = lax.dot_general(activated, scaled_all, contract_tail, preferred_element_type=f32)
    half = grad_w_in.shape[0] // 2
    sent = jnp.stack([grad_w_in[half:].astype(bf16), grad_w_out[half:].astype(bf16)])
    kept = jnp.stack([grad_w_in[:half], grad_w_out[:half]])
    block_out, image_grad, small, grads = finish(
        n,
        part,
        (
            split(branch_part),
            split(normed_part.astype(bf16)),
            stats,
            sent,
            kept,
            mixed_in,
            padded,
            image_rows,
            cotan_rows,
            taps,
            jnp.broadcast_to(ln_gain[:, None], (channels, breadth)),
            jnp.broadcast_to(layer_scale[:, None], (channels, breadth)),
        ),
        half // 2,
    )
    return (
        jnp.transpose(block_out, (1, 0, 2))[:, None],
        jnp.transpose(image_grad, (1, 0, 2))[:, None],
        small[:, : KSIZE * KSIZE].reshape(channels, KSIZE, KSIZE),
        small[:, KSIZE * KSIZE],
        small[:, KSIZE * KSIZE + 1],
        grads[0].T,
        grads[1],
    )


def solution(mesh):
    return jax.shard_map(
        body,
        mesh=mesh,
        in_specs=(
            P("chan", None, "rows", None),
            P("chan", None, None),
            P("chan"),
            P(None, "chan"),
            P("chan", None),
            P("chan"),
            P("chan", None, "rows", None),
        ),
        out_specs=(
            P("chan", None, "rows", None),
            P("chan", None, "rows", None),
            P("chan", None, None),
            P("chan"),
            P("chan"),
            P(None, "chan"),
            P("chan", None),
        ),
        check_vma=False,
    )
```

```python
import functools

import jax
import jax.numpy as jnp
from jax import lax
from jax.experimental import pallas as pl
from jax.experimental.pallas import tpu as pltpu
from jax.sharding import PartitionSpec as P

D = 768
KSIZE = 7


epsilon = 1e-06
inv_root_two = 0.7071067811865476
inv_root_two_pi = 0.3989422804014327


def gelu_slope(values):
    return (
        0.5 * (1.0 + lax.erf(values * inv_root_two))
        + values * jnp.exp(-0.5 * values * values) * inv_root_two_pi
    )


GROUP = 4
MESH = pl.DeviceIdType.MESH


def shifted(value, shift):
    if shift == 0:
        return value
    breadth = value.shape[1]
    lane = lax.broadcasted_iota(jnp.int32, value.shape, 1)
    rolled = pltpu.roll(value, shift % breadth, 1)
    keep = lane >= shift if shift > 0 else lane < breadth + shift
    return jnp.where(keep, rolled, 0.0)


def flipped(index, bit):
    return index + bit - 2 * bit * lax.rem(lax.div(index, bit), 2)


def finish_kernel(
    n,
    rows,
    part,
    branch_ref,
    normed_ref,
    stats_ref,
    sent_ref,
    kept_ref,
    mixed_ref,
    padded_ref,
    image_ref,
    cotan_ref,
    taps_ref,
    gain_ref,
    scale_ref,
    block_ref,
    image_grad_ref,
    small_ref,
    grads_ref,
    branch_in,
    normed_in,
    stats_in,
    core_in,
    near_out,
    near_in,
    row_out,
    row_in,
    grad_pad,
    running,
    sums_one,
    sums_two,
    halo_out,
    halo_in,
    small_out,
    small_in,
    local_sem,
    send_sem,
    recv_sem,
    pair_send,
    pair_recv,
):
    f32, bf16 = jnp.float32, jnp.bfloat16
    me = lax.axis_index("chan")
    row = lax.axis_index("rows")
    plane = lax.div(me, GROUP)
    lines = pl.ds(lax.rem(me, GROUP) * part, part)
    height, channels, breadth = mixed_ref.shape
    planes = n // GROUP
    steps = row_out.shape[0]
    hidden = grads_ref.shape[1]
    up, down = lax.rem(row + rows - 1, rows), lax.rem(row + 1, rows)
    partners = [flipped(row, 2**s) for s in range(steps)]

    barrier = pltpu.get_barrier_semaphore()
    for k in range(1, n):
        pl.semaphore_signal(
            barrier, inc=1, device_id={"chan": lax.rem(me + k, n)}, device_id_type=MESH
        )
    for other in [up, down] + partners:
        pl.semaphore_signal(barrier, inc=1, device_id={"rows": other}, device_id_type=MESH)
    pl.semaphore_wait(barrier, n + 1 + steps)

    def pair(index, source, target, device):
        copy = pltpu.make_async_remote_copy(
            src_ref=source,
            dst_ref=target,
            send_sem=pair_send.at[index],
            recv_sem=pair_recv.at[index],
            device_id=device,
            device_id_type=MESH,
        )
        copy.start()
        return copy

    def scatter(a, piece, target):
        copies = []
        for k in range(1, n):
            peer = lax.rem(me + k, n)
            copy = pltpu.make_async_remote_copy(
                src_ref=piece(peer),
                dst_ref=target.at[plane, lines],
                send_sem=send_sem.at[a, k],
                recv_sem=recv_sem.at[a, k],
                device_id={"chan": peer},
                device_id_type=MESH,
            )
            copy.start()
            copies.append(copy)
        copy = pltpu.make_async_copy(piece(me), target.at[plane, lines], local_sem.at[a])
        copy.start()
        return copies + [copy]

    first = scatter(0, lambda peer: stats_ref, stats_in)
    first += scatter(1, lambda peer: normed_ref.at[:, peer], normed_in)
    core = pair(0, sent_ref, core_in, {"chan": flipped(me, 1)})
    core.wait()

    @pl.loop(0, hidden // 16)
    def _(i):
        for a in range(2):
            own = pl.ds(pl.multiple_of(16 * i, 16), 16)
            other = pl.ds(pl.multiple_of(hidden + 16 * i, 16), 16)
            grads_ref[a, own, :] = kept_ref[a, own, :] + core_in[a, own, :].astype(f32)
            near_out[a, own, :] = (
                kept_ref[a, other, :] + core_in[a, other, :].astype(f32)
            ).astype(bf16)

    near = pair(1, near_out, near_in, {"chan": flipped(me, 2)})
    for copy in first:
        copy.wait()
    last = scatter(2, lambda peer: branch_ref.at[:, peer], branch_in)

    sums_one[...] = jnp.zeros_like(sums_one)
    sums_two[...] = jnp.zeros_like(sums_two)

    def normalize(start, stop):
        @pl.loop(start, stop)
        def _(r):
            grad_normed = normed_in[0, r].astype(f32)
            stats = stats_in[0, r]
            centre, inv_scale = stats[2:3], stats[3:4]
            for p in range(1, planes):
                grad_normed += normed_in[p, r].astype(f32)
                stats += stats_in[p, r]
            unit = (mixed_ref[r].astype(f32) - centre) * inv_scale
            sums_one[...] += grad_normed * unit
            scaled_grad = grad_normed * gain_ref[...]
            mixed_grad = inv_scale * (
                scaled_grad - stats[0:1] * (1.0 / D) - unit * (stats[1:2] * (1.0 / D))
            )
            grad_pad[r + 3] = mixed_grad.astype(bf16).astype(f32)

    normalize(0, 3)
    normalize(height - 3, height)
    for i in range(3):
        halo_out[0, i] = grad_pad[3 + i].astype(bf16)
        halo_out[1, i] = grad_pad[height + i].astype(bf16)
    halos = [
        pair(2, halo_out.at[0], halo_in.at[1], {"rows": up}),
        pair(3, halo_out.at[1], halo_in.at[0], {"rows": down}),
    ]
    normalize(3, height - 3)
    near.wait()

    @pl.loop(0, hidden // 16)
    def _(i):
        for a in range(2):
            own = pl.ds(pl.multiple_of(16 * i, 16), 16)
            row_out[0, a, own, :] = (grads_ref[a, own, :] + near_in[a, own, :].astype(f32)).astype(
                bf16
            )

    step = pair(4, row_out.at[0], row_in.at[0], {"rows": partners[0]})
    for copy in halos:
        copy.wait()
    above = jnp.where(row > 0, 1.0, 0.0).astype(f32)
    below = jnp.where(row < rows - 1, 1.0, 0.0).astype(f32)
    for i in range(3):
        grad_pad[i] = halo_in[0, i].astype(f32) * above
        grad_pad[height + 3 + i] = halo_in[1, i].astype(f32) * below

    @pl.loop(0, channels // 8)
    def _(g):
        group = pl.ds(pl.multiple_of(8 * g, 8), 8)
        taps = taps_ref[group, :]
        lane = lax.broadcasted_iota(jnp.int32, taps.shape, 1)
        taps_grad = jnp.zeros_like(taps)
        sums = [None] * height
        for v in range(KSIZE):
            shifts = [shifted(grad_pad[r, group, :], v - 3) for r in range(height + 6)]
            for u in range(KSIZE):
                t = u * KSIZE + v
                tap = jnp.broadcast_to(taps[:, t : t + 1], taps.shape)
                for r in range(height):
                    term = tap * shifts[r + 6 - u]
                    sums[r] = term if sums[r] is None else sums[r] + term
                both = [shifts[r + 3] * padded_ref[r + u, group, :] for r in range(height)]
                while len(both) > 1:
                    both = [p + q for p, q in zip(both[::2], both[1::2])] + both[
                        len(both) // 2 * 2 :
                    ]
                taps_grad = jnp.where(
                    lane == t, jnp.sum(both[0], axis=1, keepdims=True), taps_grad
                )
        for r in range(height):
            running[r, group, :] = sums[r]
        small_ref[group, :] = taps_grad

    @pl.loop(0, height)
    def _(r):
        image_grad_ref[r] = (running[r] + cotan_ref[r].astype(f32)).astype(bf16)

    for s in range(steps):
        step.wait()
        final = s == steps - 1

        @pl.loop(0, hidden // 16)
        def _(i):
            for a in range(2):
                own = pl.ds(pl.multiple_of(16 * i, 16), 16)
                total = row_out[s, a, own, :].astype(f32) + row_in[s, a, own, :].astype(f32)
                if final:
                    grads_ref[a, own, :] = total
                else:
                    row_out[s + 1, a, own, :] = total.astype(bf16)

        if not final:
            step = pair(
                5 + s, row_out.at[s + 1], row_in.at[s + 1], {"rows": partners[s + 1]}
            )
    for copy in last:
        copy.wait()

    @pl.loop(0, height)
    def _(r):
        branch = branch_in[0, r].astype(f32)
        for p in range(1, planes):
            branch += branch_in[p, r].astype(f32)
        sums_two[...] += branch * cotan_ref[r].astype(f32)
        block_ref[r] = (image_ref[r].astype(f32) + scale_ref[...] * branch).astype(bf16)

    lane = lax.broadcasted_iota(jnp.int32, small_ref.shape, 1)
    small = small_ref[...]
    small = jnp.where(lane == KSIZE * KSIZE, jnp.sum(sums_one[...], axis=1, keepdims=True), small)
    small = jnp.where(
        lane == KSIZE * KSIZE + 1, jnp.sum(sums_two[...], axis=1, keepdims=True), small
    )
    for s in range(steps):
        small_out[s] = small
        step = pair(4 + steps + s, small_out.at[s], small_in.at[s], {"rows": partners[s]})
        step.wait()
        small = small + small_in[s]
    small_ref[...] = small


def finish(n, part, arrays, hidden):
    f32, bf16 = jnp.float32, jnp.bfloat16
    height, channels, breadth = arrays[5].shape
    width = arrays[3].shape[2]
    planes = n // GROUP
    rows = lax.axis_size("rows")
    steps = rows.bit_length() - 1
    pairs = 4 + 2 * steps
    vmem = pl.BlockSpec(memory_space=pltpu.VMEM)
    hbm = pl.BlockSpec(memory_space=pl.ANY)
    dma = pltpu.SemaphoreType.DMA
    return pl.pallas_call(
        functools.partial(finish_kernel, n, rows, part),
        out_shape=(
            jax.ShapeDtypeStruct((height, channels, breadth), bf16),
            jax.ShapeDtypeStruct((height, channels, breadth), bf16),
            jax.ShapeDtypeStruct((channels, 128), f32),
            jax.ShapeDtypeStruct((2, hidden, width), f32),
        ),
        in_specs=[hbm] * 4 + [vmem] * 8,
        out_specs=(vmem, vmem, vmem, vmem),
        scratch_shapes=[
            pltpu.VMEM((planes, height, channels, breadth), bf16),
            pltpu.VMEM((planes, height, channels, breadth), bf16),
            pltpu.VMEM((planes, height, 4, breadth), f32),
            pltpu.VMEM((2, 2 * hidden, width), bf16),
            pltpu.VMEM((2, hidden, width), bf16),
            pltpu.VMEM((2, hidden, width), bf16),
            pltpu.VMEM((steps, 2, hidden, width), bf16),
            pltpu.VMEM((steps, 2, hidden, width), bf16),
            pltpu.VMEM((height + 6, channels, breadth), f32),
            pltpu.VMEM((height, channels, breadth), f32),
            pltpu.VMEM((channels, breadth), f32),
            pltpu.VMEM((channels, breadth), f32),
            pltpu.VMEM((2, 3, channels, breadth), bf16),
            pltpu.VMEM((2, 3, channels, breadth), bf16),
            pltpu.VMEM((steps, channels, 128), f32),
            pltpu.VMEM((steps, channels, 128), f32),
            dma((3,)),
            dma((3, n)),
            dma((3, n)),
            dma((pairs,)),
            dma((pairs,)),
        ],
        compiler_params=pltpu.CompilerParams(
            collective_id=1, has_side_effects=True, vmem_limit_bytes=36 * 2**20
        ),
        cost_estimate=pl.CostEstimate(
            flops=40000000, bytes_accessed=100000000, transcendentals=0
        ),
    )(*arrays)


def lead_kernel(
    n,
    rows,
    part,
    image_ref,
    taps_ref,
    scaled_ref,
    gain_ref,
    weights_ref,
    mixed_all,
    scaled_all,
    gain_all,
    weights_all,
    padded_ref,
    mixed_ref,
    running,
    halo_in,
    local_sem,
    send_sem,
    recv_sem,
    pair_send,
    pair_recv,
):
    f32, bf16 = jnp.float32, jnp.bfloat16
    me = lax.axis_index("chan")
    row = lax.axis_index("rows")
    height, channels, breadth = image_ref.shape
    hidden = weights_ref.shape[1]
    up, down = lax.rem(row + rows - 1, rows), lax.rem(row + 1, rows)

    barrier = pltpu.get_barrier_semaphore()
    for k in range(1, n):
        pl.semaphore_signal(
            barrier, inc=1, device_id={"chan": lax.rem(me + k, n)}, device_id_type=MESH
        )
    for other in [up, down]:
        pl.semaphore_signal(barrier, inc=1, device_id={"rows": other}, device_id_type=MESH)
    pl.semaphore_wait(barrier, n + 1)

    def pair(index, source, target, device):
        copy = pltpu.make_async_remote_copy(
            src_ref=source,
            dst_ref=target,
            send_sem=pair_send.at[index],
            recv_sem=pair_recv.at[index],
            device_id=device,
            device_id_type=MESH,
        )
        copy.start()
        return copy

    def scatter(a, piece, target):
        copies = []
        for k in range(1, n):
            peer = lax.rem(me + k, n)
            copy = pltpu.make_async_remote_copy(
                src_ref=piece(peer),
                dst_ref=target.at[:, me],
                send_sem=send_sem.at[a, k],
                recv_sem=recv_sem.at[a, k],
                device_id={"chan": peer},
                device_id_type=MESH,
            )
            copy.start()
            copies.append(copy)
        copy = pltpu.make_async_copy(piece(me), target.at[:, me], local_sem.at[a])
        copy.start()
        return copies + [copy]

    def lines(peer):
        return pl.ds(lax.rem(peer, GROUP) * part, part)

    def block(index):
        return weights_all.at[:, pl.ds(index * hidden, hidden)]

    halos = [
        pair(0, image_ref.at[pl.ds(0, 3)], halo_in.at[1], {"rows": up}),
        pair(1, image_ref.at[pl.ds(height - 3, 3)], halo_in.at[0], {"rows": down}),
    ]
    near = pair(2, weights_ref, block(1), {"chan": flipped(me, 2)})
    core = pair(3, weights_ref, block(2), {"chan": flipped(me, 1)})
    own = pltpu.make_async_copy(weights_ref, block(0), local_sem.at[3])
    own.start()
    copies = scatter(0, lambda peer: scaled_ref.at[lines(peer)], scaled_all)
    copies += scatter(1, lambda peer: gain_ref, gain_all)

    @pl.loop(0, height)
    def _(r):
        padded_ref[r + 3] = image_ref[r].astype(f32)

    for copy in halos:
        copy.wait()
    above = jnp.where(row > 0, 1.0, 0.0).astype(f32)
    below = jnp.where(row < rows - 1, 1.0, 0.0).astype(f32)
    for i in range(3):
        padded_ref[i] = halo_in[0, i].astype(f32) * above
        padded_ref[height + 3 + i] = halo_in[1, i].astype(f32) * below

    @pl.loop(0, channels // 8)
    def _(g):
        group = pl.ds(pl.multiple_of(8 * g, 8), 8)
        taps = taps_ref[group, :]
        sums = [None] * height
        for v in range(KSIZE):
            shifts = [shifted(padded_ref[r, group, :], 3 - v) for r in range(height + 6)]
            for u in range(KSIZE):
                t = u * KSIZE + v
                tap = jnp.broadcast_to(taps[:, t : t + 1], taps.shape)
                for r in range(height):
                    term = tap * shifts[r + u]
                    sums[r] = term if sums[r] is None else sums[r] + term
        for r in range(height):
            running[r, group, :] = sums[r]

    @pl.loop(0, height)
    def _(r):
        mixed_ref[r] = running[r].astype(bf16)

    copies += scatter(2, lambda peer: mixed_ref.at[lines(peer)], mixed_all)
    near.wait()
    far = pair(4, block(1), block(3), {"chan": flipped(me, 1)})
    for copy in copies + [own, core, far]:
        copy.wait()


def lead(n, part, arrays):
    f32, bf16 = jnp.float32, jnp.bfloat16
    height, channels, breadth = arrays[0].shape
    hidden, width = arrays[4].shape[1:]
    rows = lax.axis_size("rows")
    vmem = pl.BlockSpec(memory_space=pltpu.VMEM)
    hbm = pl.BlockSpec(memory_space=pl.ANY)
    dma = pltpu.SemaphoreType.DMA
    return pl.pallas_call(
        functools.partial(lead_kernel, n, rows, part),
        out_shape=(
            jax.ShapeDtypeStruct((part, n, channels, breadth), bf16),
            jax.ShapeDtypeStruct((part, n, channels, breadth), bf16),
            jax.ShapeDtypeStruct((1, n, 1, 128), f32),
            jax.ShapeDtypeStruct((2, GROUP * hidden, width), bf16),
            jax.ShapeDtypeStruct((height + 6, channels, breadth), f32),
            jax.ShapeDtypeStruct((height, channels, breadth), bf16),
        ),
        in_specs=[vmem, vmem, hbm, hbm, hbm],
        out_specs=(hbm, hbm, hbm, hbm, vmem, vmem),
        scratch_shapes=[
            pltpu.VMEM((height, channels, breadth), f32),
            pltpu.VMEM((2, 3, channels, breadth), bf16),
            dma((4,)),
            dma((3, n)),
            dma((3, n)),
            dma((5,)),
            dma((5,)),
        ],
        compiler_params=pltpu.CompilerParams(collective_id=0, has_side_effects=True),
        cost_estimate=pl.CostEstimate(
            flops=20000000, bytes_accessed=100000000, transcendentals=0
        ),
    )(*arrays)


def body(image, dw_kernel, ln_gain, w_in, w_out, layer_scale, cotangent):
    channels, images, height, breadth = image.shape
    part = height // GROUP
    n = lax.axis_size("chan")
    every = n * channels
    planes = n // GROUP
    contract_lead = (((0,), (0,)), ((), ()))
    contract_tail = (((1,), (1,)), ((), ()))
    bf16, f32 = jnp.bfloat16, jnp.float32
    image_rows = jnp.transpose(image[:, 0], (1, 0, 2))
    cotan_rows = jnp.transpose(cotangent[:, 0], (1, 0, 2))
    taps = jnp.pad(dw_kernel.reshape(channels, KSIZE * KSIZE), ((0, 0), (0, 128 - KSIZE * KSIZE)))
    scaled = (layer_scale[:, None] * cotan_rows.astype(f32)).astype(bf16)
    gain_row = jnp.pad(ln_gain[None, None, :], ((0, 0), (0, 0), (0, 128 - channels)))
    mixed_all, scaled_all, gain_all, weights, padded, mixed_in = lead(
        n, part, (image_rows, taps, scaled, gain_row, jnp.stack([w_in.T, w_out]))
    )

    def flat(value):
        value = value.reshape(part, every, breadth)
        return jnp.concatenate([value[i] for i in range(part)], axis=1)

    def split(value):
        value = jnp.stack([value[:, i * breadth : (i + 1) * breadth] for i in range(part)])
        return value.reshape(part, n, channels, breadth)

    mixed_all = flat(mixed_all).astype(f32)
    scaled_all = flat(scaled_all)
    gain_all = gain_all[0, :, 0, :channels].reshape(every, 1)
    centre = jnp.mean(mixed_all, axis=0)
    spread = jnp.mean(jnp.square(mixed_all - centre), axis=0)
    inv_scale = lax.rsqrt(spread + epsilon)
    unit_all = (mixed_all - centre) * inv_scale
    normed = (unit_all * gain_all).astype(bf16)
    pre_act = jnp.dot(weights[0], normed, preferred_element_type=f32)
    grad_act = jnp.dot(weights[1], scaled_all, preferred_element_type=f32)
    activated = jax.nn.gelu(pre_act, approximate=False).astype(bf16)
    grad_pre = (grad_act * gelu_slope(pre_act)).astype(bf16)
    branch_part = lax.dot_general(
        weights[1], activated, contract_lead, preferred_element_type=f32
    ).astype(bf16)
    normed_part = lax.dot_general(weights[0], grad_pre, contract_lead, preferred_element_type=f32)
    gained_part = normed_part * gain_all
    stats = jnp.stack(
        [jnp.sum(gained_part, axis=0), jnp.sum(gained_part * unit_all, axis=0), centre, inv_scale]
    )
    stats = jnp.transpose(stats.reshape(4, part, breadth), (1, 0, 2))
    grad_w_in = lax.dot_general(grad_pre, normed, contract_tail, preferred_element_type=f32)
    grad_w_out = lax.dot_general(activated, scaled_all, contract_tail, preferred_element_type=f32)
    half = grad_w_in.shape[0] // 2
    sent = jnp.stack([grad_w_in[half:].astype(bf16), grad_w_out[half:].astype(bf16)])
    kept = jnp.stack([grad_w_in[:half], grad_w_out[:half]])
    block_out, image_grad, small, grads = finish(
        n,
        part,
        (
            split(branch_part),
            split(normed_part.astype(bf16)),
            stats,
            sent,
            kept,
            mixed_in,
            padded,
            image_rows,
            cotan_rows,
            taps,
            jnp.broadcast_to(ln_gain[:, None], (channels, breadth)),
            jnp.broadcast_to(layer_scale[:, None], (channels, breadth)),
        ),
        half // 2,
    )
    return (
        jnp.transpose(block_out, (1, 0, 2))[:, None],
        jnp.transpose(image_grad, (1, 0, 2))[:, None],
        small[:, : KSIZE * KSIZE].reshape(channels, KSIZE, KSIZE),
        small[:, KSIZE * KSIZE],
        small[:, KSIZE * KSIZE + 1],
        grads[0].T,
        grads[1],
    )


def solution(mesh):
    return jax.shard_map(
        body,
        mesh=mesh,
        in_specs=(
            P("chan", None, "rows", None),
            P("chan", None, None),
            P("chan"),
            P(None, "chan"),
            P("chan", None),
            P("chan"),
            P("chan", None, "rows", None),
        ),
        out_specs=(
            P("chan", None, "rows", None),
            P("chan", None, "rows", None),
            P("chan", None, None),
            P("chan"),
            P("chan"),
            P(None, "chan"),
            P("chan", None),
        ),
        check_vma=False,
    )
```

```python
import functools

import jax
import jax.numpy as jnp
from jax import lax
from jax.experimental import pallas as pl
from jax.experimental.pallas import tpu as pltpu
from jax.sharding import PartitionSpec as P

D = 768
KSIZE = 7


epsilon = 1e-06
inv_root_two = 0.7071067811865476
inv_root_two_pi = 0.3989422804014327


def gelu_slope(values):
    return (
        0.5 * (1.0 + lax.erf(values * inv_root_two))
        + values * jnp.exp(-0.5 * values * values) * inv_root_two_pi
    )


GROUP = 4
MESH = pl.DeviceIdType.MESH


def shifted(value, shift):
    if shift == 0:
        return value
    breadth = value.shape[1]
    lane = lax.broadcasted_iota(jnp.int32, value.shape, 1)
    rolled = pltpu.roll(value, shift % breadth, 1)
    keep = lane >= shift if shift > 0 else lane < breadth + shift
    return jnp.where(keep, rolled, 0.0)


def flipped(index, bit):
    return index + bit - 2 * bit * lax.rem(lax.div(index, bit), 2)


def finish_kernel(
    n,
    rows,
    part,
    branch_ref,
    normed_ref,
    stats_ref,
    sent_ref,
    kept_ref,
    mixed_ref,
    padded_ref,
    image_ref,
    cotan_ref,
    taps_ref,
    block_ref,
    image_grad_ref,
    small_ref,
    grads_ref,
    branch_in,
    normed_in,
    stats_in,
    core_in,
    near_out,
    near_in,
    row_out,
    row_in,
    grad_pad,
    running,
    sums_one,
    sums_two,
    halo_out,
    halo_in,
    small_out,
    small_in,
    local_sem,
    send_sem,
    recv_sem,
    pair_send,
    pair_recv,
):
    f32, bf16 = jnp.float32, jnp.bfloat16
    me = lax.axis_index("chan")
    row = lax.axis_index("rows")
    plane = lax.div(me, GROUP)
    lines = pl.ds(lax.rem(me, GROUP) * part, part)
    height, channels, breadth = mixed_ref.shape
    planes = n // GROUP
    steps = row_out.shape[0]
    hidden = grads_ref.shape[1]
    up, down = lax.rem(row + rows - 1, rows), lax.rem(row + 1, rows)
    partners = [flipped(row, 2**s) for s in range(steps)]

    barrier = pltpu.get_barrier_semaphore()
    for k in range(1, n):
        pl.semaphore_signal(
            barrier, inc=1, device_id={"chan": lax.rem(me + k, n)}, device_id_type=MESH
        )
    for other in [up, down] + partners:
        pl.semaphore_signal(barrier, inc=1, device_id={"rows": other}, device_id_type=MESH)
    pl.semaphore_wait(barrier, n + 1 + steps)

    def pair(index, source, target, device):
        copy = pltpu.make_async_remote_copy(
            src_ref=source,
            dst_ref=target,
            send_sem=pair_send.at[index],
            recv_sem=pair_recv.at[index],
            device_id=device,
            device_id_type=MESH,
        )
        copy.start()
        return copy

    def scatter(a, piece, target):
        copies = []
        for k in range(1, n):
            peer = lax.rem(me + k, n)
            copy = pltpu.make_async_remote_copy(
                src_ref=piece(peer),
                dst_ref=target.at[plane, lines],
                send_sem=send_sem.at[a, k],
                recv_sem=recv_sem.at[a, k],
                device_id={"chan": peer},
                device_id_type=MESH,
            )
            copy.start()
            copies.append(copy)
        copy = pltpu.make_async_copy(piece(me), target.at[plane, lines], local_sem.at[a])
        copy.start()
        return copies + [copy]

    first = scatter(0, lambda peer: stats_ref, stats_in)
    first += scatter(1, lambda peer: normed_ref.at[:, peer], normed_in)
    core = pair(0, sent_ref, core_in, {"chan": flipped(me, 1)})
    core.wait()

    @pl.loop(0, hidden // 16)
    def _(i):
        for a in range(2):
            own = pl.ds(pl.multiple_of(16 * i, 16), 16)
            other = pl.ds(pl.multiple_of(hidden + 16 * i, 16), 16)
            grads_ref[a, own, :] = kept_ref[a, own, :] + core_in[a, own, :].astype(f32)
            near_out[a, own, :] = (
                kept_ref[a, other, :] + core_in[a, other, :].astype(f32)
            ).astype(bf16)

    near = pair(1, near_out, near_in, {"chan": flipped(me, 2)})
    near.wait()

    @pl.loop(0, hidden // 16)
    def _(i):
        for a in range(2):
            own = pl.ds(pl.multiple_of(16 * i, 16), 16)
            row_out[0, a, own, :] = (grads_ref[a, own, :] + near_in[a, own, :].astype(f32)).astype(
                bf16
            )

    step = pair(4, row_out.at[0], row_in.at[0], {"rows": partners[0]})
    for copy in first:
        copy.wait()
    last = scatter(2, lambda peer: branch_ref.at[:, peer], branch_in)

    extra = KSIZE * KSIZE
    gain = jnp.broadcast_to(taps_ref[:, extra : extra + 1], sums_one.shape)
    scale = jnp.broadcast_to(taps_ref[:, extra + 1 : extra + 2], sums_one.shape)
    sums_one[...] = jnp.zeros_like(sums_one)
    sums_two[...] = jnp.zeros_like(sums_two)

    def normalize(start, stop):
        @pl.loop(start, stop)
        def _(r):
            grad_normed = normed_in[0, r].astype(f32)
            stats = stats_in[0, r]
            centre, inv_scale = stats[2:3], stats[3:4]
            for p in range(1, planes):
                grad_normed += normed_in[p, r].astype(f32)
                stats += stats_in[p, r]
            unit = (mixed_ref[r].astype(f32) - centre) * inv_scale
            sums_one[...] += grad_normed * unit
            scaled_grad = grad_normed * gain
            mixed_grad = inv_scale * (
                scaled_grad - stats[0:1] * (1.0 / D) - unit * (stats[1:2] * (1.0 / D))
            )
            grad_pad[r + 3] = mixed_grad.astype(bf16).astype(f32)

    normalize(0, 3)
    normalize(height - 3, height)
    for i in range(3):
        halo_out[0, i] = grad_pad[3 + i].astype(bf16)
        halo_out[1, i] = grad_pad[height + i].astype(bf16)
    halos = [
        pair(2, halo_out.at[0], halo_in.at[1], {"rows": up}),
        pair(3, halo_out.at[1], halo_in.at[0], {"rows": down}),
    ]
    normalize(3, height - 3)
    for copy in halos:
        copy.wait()
    above = jnp.where(row > 0, 1.0, 0.0).astype(f32)
    below = jnp.where(row < rows - 1, 1.0, 0.0).astype(f32)
    for i in range(3):
        grad_pad[i] = halo_in[0, i].astype(f32) * above
        grad_pad[height + 3 + i] = halo_in[1, i].astype(f32) * below

    @pl.loop(0, channels // 8)
    def _(g):
        group = pl.ds(pl.multiple_of(8 * g, 8), 8)
        taps = taps_ref[group, :]
        lane = lax.broadcasted_iota(jnp.int32, taps.shape, 1)
        taps_grad = jnp.zeros_like(taps)
        sums = [None] * height
        for v in range(KSIZE):
            shifts = [shifted(grad_pad[r, group, :], v - 3) for r in range(height + 6)]
            for u in range(KSIZE):
                t = u * KSIZE + v
                tap = jnp.broadcast_to(taps[:, t : t + 1], taps.shape)
                for r in range(height):
                    term = tap * shifts[r + 6 - u]
                    sums[r] = term if sums[r] is None else sums[r] + term
                both = [shifts[r + 3] * padded_ref[r + u, group, :] for r in range(height)]
                while len(both) > 1:
                    both = [p + q for p, q in zip(both[::2], both[1::2])] + both[
                        len(both) // 2 * 2 :
                    ]
                taps_grad = jnp.where(
                    lane == t, jnp.sum(both[0], axis=1, keepdims=True), taps_grad
                )
        for r in range(height):
            running[r, group, :] = sums[r]
        small_ref[group, :] = taps_grad

    @pl.loop(0, height)
    def _(r):
        image_grad_ref[r] = (running[r] + cotan_ref[r].astype(f32)).astype(bf16)

    for s in range(steps):
        step.wait()
        final = s == steps - 1

        @pl.loop(0, hidden // 16)
        def _(i):
            for a in range(2):
                own = pl.ds(pl.multiple_of(16 * i, 16), 16)
                total = row_out[s, a, own, :].astype(f32) + row_in[s, a, own, :].astype(f32)
                if final:
                    grads_ref[a, own, :] = total
                else:
                    row_out[s + 1, a, own, :] = total.astype(bf16)

        if not final:
            step = pair(
                5 + s, row_out.at[s + 1], row_in.at[s + 1], {"rows": partners[s + 1]}
            )
    for copy in last:
        copy.wait()

    @pl.loop(0, height)
    def _(r):
        branch = branch_in[0, r].astype(f32)
        for p in range(1, planes):
            branch += branch_in[p, r].astype(f32)
        sums_two[...] += branch * cotan_ref[r].astype(f32)
        block_ref[r] = (image_ref[r].astype(f32) + scale * branch).astype(bf16)

    lane = lax.broadcasted_iota(jnp.int32, small_ref.shape, 1)
    small = small_ref[...]
    small = jnp.where(lane == KSIZE * KSIZE, jnp.sum(sums_one[...], axis=1, keepdims=True), small)
    small = jnp.where(
        lane == KSIZE * KSIZE + 1, jnp.sum(sums_two[...], axis=1, keepdims=True), small
    )
    for s in range(steps):
        small_out[s] = small
        step = pair(4 + steps + s, small_out.at[s], small_in.at[s], {"rows": partners[s]})
        step.wait()
        small = small + small_in[s]
    small_ref[...] = small


def finish(n, part, arrays, hidden):
    f32, bf16 = jnp.float32, jnp.bfloat16
    height, channels, breadth = arrays[5].shape
    width = arrays[3].shape[2]
    planes = n // GROUP
    rows = lax.axis_size("rows")
    steps = rows.bit_length() - 1
    pairs = 4 + 2 * steps
    vmem = pl.BlockSpec(memory_space=pltpu.VMEM)
    hbm = pl.BlockSpec(memory_space=pl.ANY)
    dma = pltpu.SemaphoreType.DMA
    return pl.pallas_call(
        functools.partial(finish_kernel, n, rows, part),
        out_shape=(
            jax.ShapeDtypeStruct((height, channels, breadth), bf16),
            jax.ShapeDtypeStruct((height, channels, breadth), bf16),
            jax.ShapeDtypeStruct((channels, 128), f32),
            jax.ShapeDtypeStruct((2, hidden, width), f32),
        ),
        in_specs=[hbm] * 4 + [vmem] * 6,
        out_specs=(vmem, vmem, vmem, vmem),
        scratch_shapes=[
            pltpu.VMEM((planes, height, channels, breadth), bf16),
            pltpu.VMEM((planes, height, channels, breadth), bf16),
            pltpu.VMEM((planes, height, 4, breadth), f32),
            pltpu.VMEM((2, 2 * hidden, width), bf16),
            pltpu.VMEM((2, hidden, width), bf16),
            pltpu.VMEM((2, hidden, width), bf16),
            pltpu.VMEM((steps, 2, hidden, width), bf16),
            pltpu.VMEM((steps, 2, hidden, width), bf16),
            pltpu.VMEM((height + 6, channels, breadth), f32),
            pltpu.VMEM((height, channels, breadth), f32),
            pltpu.VMEM((channels, breadth), f32),
            pltpu.VMEM((channels, breadth), f32),
            pltpu.VMEM((2, 3, channels, breadth), bf16),
            pltpu.VMEM((2, 3, channels, breadth), bf16),
            pltpu.VMEM((steps, channels, 128), f32),
            pltpu.VMEM((steps, channels, 128), f32),
            dma((3,)),
            dma((3, n)),
            dma((3, n)),
            dma((pairs,)),
            dma((pairs,)),
        ],
        compiler_params=pltpu.CompilerParams(
            collective_id=1, has_side_effects=True, vmem_limit_bytes=36 * 2**20
        ),
        cost_estimate=pl.CostEstimate(
            flops=40000000, bytes_accessed=100000000, transcendentals=0
        ),
    )(*arrays)


def lead_kernel(
    n,
    rows,
    part,
    image_ref,
    taps_ref,
    scaled_ref,
    gain_ref,
    weights_ref,
    mixed_all,
    scaled_all,
    gain_all,
    weights_all,
    padded_ref,
    mixed_ref,
    running,
    halo_in,
    local_sem,
    send_sem,
    recv_sem,
    pair_send,
    pair_recv,
):
    f32, bf16 = jnp.float32, jnp.bfloat16
    me = lax.axis_index("chan")
    row = lax.axis_index("rows")
    height, channels, breadth = image_ref.shape
    hidden = weights_ref.shape[1]
    up, down = lax.rem(row + rows - 1, rows), lax.rem(row + 1, rows)

    barrier = pltpu.get_barrier_semaphore()
    for k in range(1, n):
        pl.semaphore_signal(
            barrier, inc=1, device_id={"chan": lax.rem(me + k, n)}, device_id_type=MESH
        )
    for other in [up, down]:
        pl.semaphore_signal(barrier, inc=1, device_id={"rows": other}, device_id_type=MESH)
    pl.semaphore_wait(barrier, n + 1)

    def pair(index, source, target, device):
        copy = pltpu.make_async_remote_copy(
            src_ref=source,
            dst_ref=target,
            send_sem=pair_send.at[index],
            recv_sem=pair_recv.at[index],
            device_id=device,
            device_id_type=MESH,
        )
        copy.start()
        return copy

    def scatter(a, piece, target):
        copies = []
        for k in range(1, n):
            peer = lax.rem(me + k, n)
            copy = pltpu.make_async_remote_copy(
                src_ref=piece(peer),
                dst_ref=target.at[:, me],
                send_sem=send_sem.at[a, k],
                recv_sem=recv_sem.at[a, k],
                device_id={"chan": peer},
                device_id_type=MESH,
            )
            copy.start()
            copies.append(copy)
        copy = pltpu.make_async_copy(piece(me), target.at[:, me], local_sem.at[a])
        copy.start()
        return copies + [copy]

    def lines(peer):
        return pl.ds(lax.rem(peer, GROUP) * part, part)

    def block(index):
        return weights_all.at[:, pl.ds(index * hidden, hidden)]

    halos = [
        pair(0, image_ref.at[pl.ds(0, 3)], halo_in.at[1], {"rows": up}),
        pair(1, image_ref.at[pl.ds(height - 3, 3)], halo_in.at[0], {"rows": down}),
    ]
    near = pair(2, weights_ref, block(1), {"chan": flipped(me, 2)})
    core = pair(3, weights_ref, block(2), {"chan": flipped(me, 1)})
    own = pltpu.make_async_copy(weights_ref, block(0), local_sem.at[3])
    own.start()
    copies = scatter(0, lambda peer: scaled_ref.at[lines(peer)], scaled_all)
    copies += scatter(1, lambda peer: gain_ref, gain_all)

    @pl.loop(0, height)
    def _(r):
        padded_ref[r + 3] = image_ref[r].astype(f32)

    for copy in halos:
        copy.wait()
    above = jnp.where(row > 0, 1.0, 0.0).astype(f32)
    below = jnp.where(row < rows - 1, 1.0, 0.0).astype(f32)
    for i in range(3):
        padded_ref[i] = halo_in[0, i].astype(f32) * above
        padded_ref[height + 3 + i] = halo_in[1, i].astype(f32) * below

    @pl.loop(0, channels // 8)
    def _(g):
        group = pl.ds(pl.multiple_of(8 * g, 8), 8)
        taps = taps_ref[group, :]
        sums = [None] * height
        for v in range(KSIZE):
            shifts = [shifted(padded_ref[r, group, :], 3 - v) for r in range(height + 6)]
            for u in range(KSIZE):
                t = u * KSIZE + v
                tap = jnp.broadcast_to(taps[:, t : t + 1], taps.shape)
                for r in range(height):
                    term = tap * shifts[r + u]
                    sums[r] = term if sums[r] is None else sums[r] + term
        for r in range(height):
            running[r, group, :] = sums[r]

    @pl.loop(0, height)
    def _(r):
        mixed_ref[r] = running[r].astype(bf16)

    copies += scatter(2, lambda peer: mixed_ref.at[lines(peer)], mixed_all)
    near.wait()
    far = pair(4, block(1), block(3), {"chan": flipped(me, 1)})
    for copy in copies + [own, core, far]:
        copy.wait()


def lead(n, part, arrays):
    f32, bf16 = jnp.float32, jnp.bfloat16
    height, channels, breadth = arrays[0].shape
    hidden, width = arrays[4].shape[1:]
    rows = lax.axis_size("rows")
    vmem = pl.BlockSpec(memory_space=pltpu.VMEM)
    hbm = pl.BlockSpec(memory_space=pl.ANY)
    dma = pltpu.SemaphoreType.DMA
    return pl.pallas_call(
        functools.partial(lead_kernel, n, rows, part),
        out_shape=(
            jax.ShapeDtypeStruct((part, n, channels, breadth), bf16),
            jax.ShapeDtypeStruct((part, n, channels, breadth), bf16),
            jax.ShapeDtypeStruct((1, n, 1, 128), f32),
            jax.ShapeDtypeStruct((2, GROUP * hidden, width), bf16),
            jax.ShapeDtypeStruct((height + 6, channels, breadth), f32),
            jax.ShapeDtypeStruct((height, channels, breadth), bf16),
        ),
        in_specs=[vmem, vmem, hbm, hbm, hbm],
        out_specs=(hbm, hbm, hbm, hbm, vmem, vmem),
        scratch_shapes=[
            pltpu.VMEM((height, channels, breadth), f32),
            pltpu.VMEM((2, 3, channels, breadth), bf16),
            dma((4,)),
            dma((3, n)),
            dma((3, n)),
            dma((5,)),
            dma((5,)),
        ],
        compiler_params=pltpu.CompilerParams(collective_id=0, has_side_effects=True),
        cost_estimate=pl.CostEstimate(
            flops=20000000, bytes_accessed=100000000, transcendentals=0
        ),
    )(*arrays)


def body(image, dw_kernel, ln_gain, w_in, w_out, layer_scale, cotangent):
    channels, images, height, breadth = image.shape
    part = height // GROUP
    n = lax.axis_size("chan")
    every = n * channels
    planes = n // GROUP
    contract_lead = (((0,), (0,)), ((), ()))
    contract_tail = (((1,), (1,)), ((), ()))
    bf16, f32 = jnp.bfloat16, jnp.float32
    image_rows = jnp.transpose(image[:, 0], (1, 0, 2))
    cotan_rows = jnp.transpose(cotangent[:, 0], (1, 0, 2))
    taps = jnp.concatenate(
        [
            dw_kernel.reshape(channels, KSIZE * KSIZE),
            ln_gain[:, None],
            layer_scale[:, None],
            jnp.zeros((channels, 126 - KSIZE * KSIZE), f32),
        ],
        axis=1,
    )
    scaled = (layer_scale[:, None] * cotan_rows.astype(f32)).astype(bf16)
    gain_row = jnp.pad(ln_gain[None, None, :], ((0, 0), (0, 0), (0, 128 - channels)))
    mixed_all, scaled_all, gain_all, weights, padded, mixed_in = lead(
        n, part, (image_rows, taps, scaled, gain_row, jnp.stack([w_in.T, w_out]))
    )

    def flat(value):
        value = value.reshape(part, every, breadth)
        return jnp.concatenate([value[i] for i in range(part)], axis=1)

    def split(value):
        value = jnp.stack([value[:, i * breadth : (i + 1) * breadth] for i in range(part)])
        return value.reshape(part, n, channels, breadth)

    mixed_all = flat(mixed_all).astype(f32)
    scaled_all = flat(scaled_all)
    gain_all = gain_all[0, :, 0, :channels].reshape(every, 1)
    centre = jnp.mean(mixed_all, axis=0)
    spread = jnp.mean(jnp.square(mixed_all - centre), axis=0)
    inv_scale = lax.rsqrt(spread + epsilon)
    unit_all = (mixed_all - centre) * inv_scale
    normed = (unit_all * gain_all).astype(bf16)
    pre_act = jnp.dot(weights[0], normed, preferred_element_type=f32)
    grad_act = jnp.dot(weights[1], scaled_all, preferred_element_type=f32)
    activated = jax.nn.gelu(pre_act, approximate=False).astype(bf16)
    grad_pre = (grad_act * gelu_slope(pre_act)).astype(bf16)
    branch_part = lax.dot_general(
        weights[1], activated, contract_lead, preferred_element_type=f32
    ).astype(bf16)
    normed_part = lax.dot_general(weights[0], grad_pre, contract_lead, preferred_element_type=f32)
    gained_part = normed_part * gain_all
    stats = jnp.stack(
        [jnp.sum(gained_part, axis=0), jnp.sum(gained_part * unit_all, axis=0), centre, inv_scale]
    )
    stats = jnp.transpose(stats.reshape(4, part, breadth), (1, 0, 2))
    grad_w_in = lax.dot_general(grad_pre, normed, contract_tail, preferred_element_type=f32)
    grad_w_out = lax.dot_general(activated, scaled_all, contract_tail, preferred_element_type=f32)
    half = grad_w_in.shape[0] // 2
    sent = jnp.stack([grad_w_in[half:].astype(bf16), grad_w_out[half:].astype(bf16)])
    kept = jnp.stack([grad_w_in[:half], grad_w_out[:half]])
    block_out, image_grad, small, grads = finish(
        n,
        part,
        (
            split(branch_part),
            split(normed_part.astype(bf16)),
            stats,
            sent,
            kept,
            mixed_in,
            padded,
            image_rows,
            cotan_rows,
            taps,
        ),
        half // 2,
    )
    return (
        jnp.transpose(block_out, (1, 0, 2))[:, None],
        jnp.transpose(image_grad, (1, 0, 2))[:, None],
        small[:, : KSIZE * KSIZE].reshape(channels, KSIZE, KSIZE),
        small[:, KSIZE * KSIZE],
        small[:, KSIZE * KSIZE + 1],
        grads[0].T,
        grads[1],
    )


def solution(mesh):
    return jax.shard_map(
        body,
        mesh=mesh,
        in_specs=(
            P("chan", None, "rows", None),
            P("chan", None, None),
            P("chan"),
            P(None, "chan"),
            P("chan", None),
            P("chan"),
            P("chan", None, "rows", None),
        ),
        out_specs=(
            P("chan", None, "rows", None),
            P("chan", None, "rows", None),
            P("chan", None, None),
            P("chan"),
            P("chan"),
            P(None, "chan"),
            P("chan", None),
        ),
        check_vma=False,
    )
```
